512 devices in a mesh: len: 128 (over y, z, core), pipe: 4 (over x).
Axes of the slice: x: 4, y: 4, z: 16, core: 2. Of those that a mesh axis runs over, the one named last changes fastest.
Arguments:
- inputs: bfloat16 [512, 2048, 256], P(('len', 'pipe')), may hold values from -6 to 6
- cotangent: bfloat16 [512, 2048, 256], P(('len', 'pipe')), may hold values from -6 to 6
- point_weight: bfloat16 [256, 256], replicated, may hold values from -0.375 to 0.375
- point_bias: float32 [256], replicated, may hold values from -3 to 3
- spec_real: bfloat16 [128, 256, 256], P('len'), may hold values from -0.25 to 0.25
- spec_imag: bfloat16 [128, 256, 256], P('len'), may hold values from -0.25 to 0.25
- junc_weight: bfloat16 [256, 256], replicated, may hold values from -0.375 to 0.375
- junc_bias: float32 [256], replicated, may hold values from -3 to 3
- inlet_ids: int32 [512], replicated, may hold values from 0 to 511
- outlet_ids: int32 [512], replicated, may hold values from 0 to 511
Outputs:
- outputs: bfloat16 [512, 2048, 256], P(('len', 'pipe'))
- grad_inputs: bfloat16 [512, 2048, 256], P(('len', 'pipe'))
- grad_real: float32 [128, 256, 256], P('len')
- grad_imag: float32 [128, 256, 256], P('len')
The draws below stay inside these ranges and needn't reach their ends.
All inputs are finite; a program needn't handle non-finite values.
Results may differ from the reference program's by a relative error of at most 0.015.
Values may be sent and summed in bfloat16 or wider, within the bound.
A program may use at most 64 MiB of HBM per device.

```python
import math
import jax
import jax.numpy as jnp
from jax import lax

C = 256
MODES = 128
CELLS = 2048
PIPES = 512
JUNCS = 512


def touch_ends(drawn, stream_key, low, top_value):
    shape = drawn.shape
    spot = [jax.random.randint(jax.random.fold_in(stream_key, axis), (), 0, shape[axis]) for axis in range(len(shape))]
    drawn = drawn.at[tuple(spot)].set(low)
    longest = shape.index(max(shape))
    spot[longest] = (spot[longest] + 1) % shape[longest]
    return drawn.at[tuple(spot)].set(top_value)


def shard_levels(own_key, extent, pieces, least, high):
    loudness, own = 1.0, jax.random.fold_in(own_key, 6)
    for axis_at, shards_of in pieces:
        heights = jnp.exp(jax.random.uniform(jax.random.fold_in(own, axis_at), (shards_of,), jnp.float32, least / len(pieces), high / len(pieces)))
        loudness = loudness * jnp.repeat(heights, extent[axis_at] // shards_of).reshape([-1 if axis == axis_at else 1 for axis in range(len(extent))])
    return loudness


def bell_draw(stream_key, shape, width, limit, shards=(), dtype=jnp.bfloat16):
    level = shard_levels(stream_key, shape, shards, -0.22, 0.18) if shards else 1.0
    entries = jax.random.normal(stream_key, shape, jnp.float32) * width * level
    return jnp.minimum(jnp.maximum(entries, -limit), limit).astype(dtype)


def setup_inputs(seed: int = 0) -> dict:
    splits = jax.random.split(jax.random.key(seed), 11)
    inputs = bell_draw(splits[0], (PIPES, CELLS, C), 1.0, 6.0, ((0, 512),))
    cotangent = bell_draw(splits[1], (PIPES, CELLS, C), 1.0, 6.0, ((0, 512),))
    point_weight = bell_draw(splits[2], (C, C), C ** -0.5, 0.375)
    point_bias = bell_draw(splits[3], (C,), 0.5, 3.0, (), jnp.float32)
    spec_real = bell_draw(splits[4], (MODES, C, C), (2 * C) ** -0.5, 0.25, ((0, 128),))
    spec_imag = bell_draw(splits[5], (MODES, C, C), (2 * C) ** -0.5, 0.25, ((0, 128),))
    junc_weight = bell_draw(splits[6], (C, C), C ** -0.5, 0.375)
    junc_bias = bell_draw(splits[7], (C,), 0.5, 3.0, (), jnp.float32)
    inlet_ids = touch_ends(jax.random.randint(splits[8], (PIPES,), 0, JUNCS), jax.random.fold_in(splits[8], 1), 0, JUNCS - 1).astype(jnp.int32)
    outlet_ids = touch_ends(jax.random.randint(splits[9], (PIPES,), 0, JUNCS), jax.random.fold_in(splits[9], 1), 0, JUNCS - 1).astype(jnp.int32)
    return dict(inputs=inputs, cotangent=cotangent, point_weight=point_weight, point_bias=point_bias, spec_real=spec_real, spec_imag=spec_imag, junc_weight=junc_weight, junc_bias=junc_bias, inlet_ids=inlet_ids, outlet_ids=outlet_ids)


COUPLING = 0.125

def tables(cell_count, mode_count):
    position = lax.broadcasted_iota(jnp.int32, (mode_count, cell_count), 1)
    frequency = lax.broadcasted_iota(jnp.int32, (mode_count, cell_count), 0)
    product_index = frequency * position % cell_count
    angles = product_index.astype(jnp.float32) * (2.0 * math.pi / cell_count)
    norm_scale = 1.0 / math.sqrt(cell_count)
    cosine = jnp.cos(angles) * norm_scale
    sine_table = jnp.sin(angles) * norm_scale
    doubled = jnp.where(frequency == 0, 1.0, 2.0)
    forward = jnp.stack([cosine, -sine_table], axis=1).reshape(2 * mode_count, cell_count).astype(jnp.bfloat16)
    inverse = jnp.transpose(jnp.stack([doubled * cosine, -doubled * sine_table], axis=1).reshape(2 * mode_count, cell_count)).astype(jnp.bfloat16)
    return (forward, inverse)

def spectral_blocks(spec_real, spec_imag):
    upper = jnp.concatenate([spec_real, spec_imag], axis=2)
    lower = jnp.concatenate([-spec_imag, spec_real], axis=2)
    return jnp.concatenate([upper, lower], axis=1)

def activate(values):
    return jax.nn.gelu(values, approximate=True)

def silu_slope(values):
    sigmoid_part = jax.nn.sigmoid(values)
    return sigmoid_part * (1.0 + values * (1.0 - sigmoid_part))

def reference(inputs, cotangent, point_weight, point_bias, spec_real, spec_imag, junc_weight, junc_bias, inlet_ids, outlet_ids):
    forward, inverse = tables(CELLS, MODES)
    forward_wide = forward.astype(jnp.float32)
    inverse_wide = inverse.astype(jnp.float32)
    blocks = spectral_blocks(spec_real, spec_imag).astype(jnp.float32)
    pipe_blocks = inputs.reshape(-1, 16, CELLS, C)

    def transform(block):
        return jnp.einsum('kl,plc->pkc', forward_wide, block.astype(jnp.float32)).astype(jnp.bfloat16)
    spectra = lax.map(transform, pipe_blocks).reshape(PIPES, MODES, 2 * C)
    mixed = jnp.einsum('pmk,mkn->pmn', spectra.astype(jnp.float32), blocks).astype(jnp.bfloat16)
    junction_iota = lax.broadcasted_iota(jnp.int32, (PIPES, JUNCS), 1)
    in_hot = (inlet_ids[:, None] == junction_iota).astype(jnp.bfloat16)
    out_hot = (outlet_ids[:, None] == junction_iota).astype(jnp.bfloat16)
    partial_value = jnp.dot(in_hot.T, inputs[:, 0, :], preferred_element_type=jnp.float32) + jnp.dot(out_hot.T, inputs[:, -1, :], preferred_element_type=jnp.float32)
    junc_act = jnp.dot(partial_value.astype(jnp.bfloat16), junc_weight, preferred_element_type=jnp.float32) + junc_bias
    junc_rows = jax.nn.silu(junc_act).astype(jnp.bfloat16)
    cond = COUPLING * (jnp.dot(in_hot, junc_rows, preferred_element_type=jnp.float32) + jnp.dot(out_hot, junc_rows, preferred_element_type=jnp.float32))
    mixed_blocks = mixed.reshape(-1, 16, 2 * MODES, C)
    cond_blocks = cond.reshape(-1, 16, C)
    cot_blocks = cotangent.reshape(-1, 16, CELLS, C)

    def forward_block(items):
        block, mode_rows, cond_rows, cot_rows = items
        spectral = jnp.einsum('lk,pkc->plc', inverse_wide, mode_rows.astype(jnp.float32))
        pre = (spectral + cond_rows[:, None, :]).astype(jnp.bfloat16)
        pointwise = jnp.dot(block.reshape(-1, C), point_weight, preferred_element_type=jnp.float32).reshape(block.shape)
        summed = pointwise + point_bias + pre.astype(jnp.float32)
        result, pullback = jax.vjp(activate, summed)
        grad_total = pullback(cot_rows.astype(jnp.float32))[0].astype(jnp.bfloat16)
        grad_spec = jnp.einsum('lk,plc->pkc', inverse_wide, grad_total.astype(jnp.float32)).astype(jnp.bfloat16)
        grad_cond = lax.optimization_barrier(jnp.sum(grad_total.astype(jnp.float32), axis=1))
        return (result.astype(jnp.bfloat16), grad_total, grad_spec, grad_cond)
    outputs, grad_total, grad_spec, grad_cond = lax.map(forward_block, (pipe_blocks, mixed_blocks, cond_blocks, cot_blocks))
    outputs = outputs.reshape(PIPES, CELLS, C)
    grad_modes = grad_spec.reshape(PIPES, MODES, 2 * C).astype(jnp.float32)
    grad_cond = grad_cond.reshape(PIPES, C)
    weight_terms = jnp.einsum('pmk,pmn->mkn', spectra.astype(jnp.float32), grad_modes)
    grad_real = weight_terms[:, :C, :C] + weight_terms[:, C:, C:]
    grad_imag = weight_terms[:, :C, C:] - weight_terms[:, C:, :C]
    grad_mixed = jnp.einsum('pmn,mkn->pmk', grad_modes, blocks).astype(jnp.bfloat16).reshape(-1, 16, 2 * MODES, C)
    in_wide = in_hot.astype(jnp.float32)
    out_wide = out_hot.astype(jnp.float32)
    junc_grad = COUPLING * (jnp.dot(in_wide.T, grad_cond, precision=lax.Precision.HIGHEST) + jnp.dot(out_wide.T, grad_cond, precision=lax.Precision.HIGHEST))
    act_grad = (junc_grad * silu_slope(junc_act)).astype(jnp.bfloat16)
    sums_grad = jnp.dot(act_grad, junc_weight.T, preferred_element_type=jnp.float32).astype(jnp.bfloat16)
    end_first = jnp.dot(in_hot, sums_grad, preferred_element_type=jnp.float32).reshape(-1, 16, C)
    end_last = jnp.dot(out_hot, sums_grad, preferred_element_type=jnp.float32).reshape(-1, 16, C)

    def backward_block(items):
        grad_rows, first_rows, last_rows, total_rows = items
        grad_cells = jnp.einsum('kl,pkc->plc', forward_wide, grad_rows.astype(jnp.float32))
        grad_cells = grad_cells.at[:, 0, :].add(first_rows).at[:, -1, :].add(last_rows)
        spread = grad_cells.astype(jnp.bfloat16)
        grad_local = jnp.dot(total_rows.reshape(-1, C), point_weight.T, preferred_element_type=jnp.float32).reshape(total_rows.shape)
        return (grad_local + spread.astype(jnp.float32)).astype(jnp.bfloat16)
    grad_inputs = lax.map(backward_block, (grad_mixed, end_first, end_last, grad_total)).reshape(PIPES, CELLS, C)
    return (outputs, grad_inputs, grad_real, grad_imag)
```

```python
import math

import jax
import jax.numpy as jnp
from jax import lax
from jax.sharding import PartitionSpec as P

COUPLING = 0.125


def tables(cell_count, mode_count):
    position = lax.broadcasted_iota(jnp.int32, (mode_count, cell_count), 1)
    frequency = lax.broadcasted_iota(jnp.int32, (mode_count, cell_count), 0)
    product_index = frequency * position % cell_count
    angles = product_index.astype(jnp.float32) * (2.0 * math.pi / cell_count)
    norm_scale = 1.0 / math.sqrt(cell_count)
    cosine = jnp.cos(angles) * norm_scale
    sine_table = jnp.sin(angles) * norm_scale
    doubled = jnp.where(frequency == 0, 1.0, 2.0)
    forward = (
        jnp.stack([cosine, -sine_table], axis=1)
        .reshape(2 * mode_count, cell_count)
        .astype(jnp.bfloat16)
    )
    inverse = jnp.transpose(
        jnp.stack([doubled * cosine, -doubled * sine_table], axis=1).reshape(
            2 * mode_count, cell_count
        )
    ).astype(jnp.bfloat16)
    return (forward, inverse)


def spectral_blocks(spec_real, spec_imag):
    upper = jnp.concatenate([spec_real, spec_imag], axis=2)
    lower = jnp.concatenate([-spec_imag, spec_real], axis=2)
    return jnp.concatenate([upper, lower], axis=1)


def activate(values):
    return jax.nn.gelu(values, approximate=True)


def silu_slope(values):
    sigmoid_part = jax.nn.sigmoid(values)
    return sigmoid_part * (1.0 + values * (1.0 - sigmoid_part))


def to_modes(field):
    return lax.all_to_all(field, "len", split_axis=1, concat_axis=0, tiled=True)


def from_modes(field):
    return lax.all_to_all(field, "len", split_axis=0, concat_axis=1, tiled=True)


def body(
    inputs,
    cotangent,
    point_weight,
    point_bias,
    spec_real,
    spec_imag,
    junc_weight,
    junc_bias,
    inlet_ids,
    outlet_ids,
):
    per_dev, cell_count, channels = inputs.shape
    len_count = lax.axis_size("len")
    mode_count = spec_real.shape[0] * len_count
    junc_count = inlet_ids.shape[0]
    forward, inverse = tables(cell_count, mode_count)
    blocks = spectral_blocks(spec_real, spec_imag)
    start = (lax.axis_index("len") * lax.axis_size("pipe") + lax.axis_index("pipe")) * per_dev
    my_inlets = lax.dynamic_slice_in_dim(inlet_ids, start, per_dev)
    my_outlets = lax.dynamic_slice_in_dim(outlet_ids, start, per_dev)
    mine = jnp.concatenate([my_inlets, my_outlets])[:, None]
    in_match = mine == inlet_ids[None, :]
    out_match = mine == outlet_ids[None, :]
    end_rows = lax.all_gather(
        jnp.stack([inputs[:, 0, :], inputs[:, -1, :]]), ("len", "pipe"), axis=1, tiled=True
    )
    spectra = jnp.einsum("kl,plc->pkc", forward, inputs, preferred_element_type=jnp.float32).astype(
        jnp.bfloat16
    )
    mode_rows = to_modes(spectra.reshape(per_dev, mode_count, 2, channels))
    mode_rows = mode_rows.reshape(mode_rows.shape[0], -1, 2 * channels)
    mixed = jnp.einsum(
        "pmk,mkn->pmn", mode_rows, blocks, preferred_element_type=jnp.float32
    ).astype(jnp.bfloat16)
    returned_modes = from_modes(mixed.reshape(mixed.shape[0], -1, 2, channels)).reshape(
        per_dev, 2 * mode_count, channels
    )

    junc_sums = jnp.dot(
        in_match.astype(jnp.bfloat16), end_rows[0], preferred_element_type=jnp.float32
    ) + jnp.dot(out_match.astype(jnp.bfloat16), end_rows[1], preferred_element_type=jnp.float32)
    junc_act = (
        jnp.dot(junc_sums.astype(jnp.bfloat16), junc_weight, preferred_element_type=jnp.float32)
        + junc_bias
    )
    junc_rows = jax.nn.silu(junc_act).astype(jnp.bfloat16).astype(jnp.float32)
    cond = COUPLING * (junc_rows[:per_dev] + junc_rows[per_dev:])
    spectral = jnp.einsum(
        "lk,pkc->plc", inverse, returned_modes, preferred_element_type=jnp.float32
    )
    pre = (spectral + cond[:, None, :]).astype(jnp.bfloat16)
    pointwise = jnp.dot(
        inputs.reshape(-1, channels), point_weight, preferred_element_type=jnp.float32
    ).reshape(inputs.shape)
    summed = pointwise + point_bias + pre.astype(jnp.float32)
    result, pullback = jax.vjp(activate, summed)
    outputs = result.astype(jnp.bfloat16)
    grad_total = pullback(cotangent.astype(jnp.float32))[0].astype(jnp.bfloat16)
    grad_spec = jnp.einsum(
        "lk,plc->pkc", inverse, grad_total, preferred_element_type=jnp.float32
    ).astype(jnp.bfloat16)
    grad_modes = to_modes(grad_spec.reshape(per_dev, mode_count, 2, channels))
    grad_modes = grad_modes.reshape(grad_modes.shape[0], -1, 2 * channels)
    grad_mixed = jnp.einsum(
        "pmn,mkn->pmk", grad_modes, blocks, preferred_element_type=jnp.float32
    ).astype(jnp.bfloat16)
    weight_terms = jnp.einsum(
        "pmk,pmn->mkn", mode_rows, grad_modes, preferred_element_type=jnp.float32
    )
    real_terms = weight_terms[:, :channels, :channels] + weight_terms[:, channels:, channels:]
    imag_terms = weight_terms[:, :channels, channels:] - weight_terms[:, channels:, :channels]
    grad_real, grad_imag = (
        jnp.sum(lax.all_gather(real_terms.astype(jnp.bfloat16), "pipe").astype(jnp.float32), axis=0),
        jnp.sum(lax.all_gather(imag_terms.astype(jnp.bfloat16), "pipe").astype(jnp.float32), axis=0),
    )
    grad_back = from_modes(grad_mixed.reshape(grad_mixed.shape[0], -1, 2, channels)).reshape(
        per_dev, 2 * mode_count, channels
    )
    grad_cells = jnp.einsum("kl,pkc->plc", forward, grad_back, preferred_element_type=jnp.float32)
    grad_cond = jnp.sum(grad_total, axis=1, dtype=jnp.float32)
    all_cond = lax.all_gather(grad_cond, ("len", "pipe"), axis=0, tiled=True)
    junc_grad = COUPLING * jnp.dot(
        in_match.astype(jnp.float32) + out_match.astype(jnp.float32),
        all_cond,
        precision=lax.Precision.HIGHEST,
    )
    act_grad = (junc_grad * silu_slope(junc_act)).astype(jnp.bfloat16)
    sums_grad = jnp.dot(act_grad, junc_weight.T, preferred_element_type=jnp.float32).astype(
        jnp.bfloat16
    )
    end_first = sums_grad[:per_dev].astype(jnp.float32)
    end_last = sums_grad[per_dev:].astype(jnp.float32)
    grad_cells = grad_cells.at[:, 0, :].add(end_first).at[:, -1, :].add(end_last)
    spread = grad_cells.astype(jnp.bfloat16)
    grad_local = jnp.dot(
        grad_total.reshape(-1, channels), point_weight.T, preferred_element_type=jnp.float32
    ).reshape(inputs.shape)
    grad_inputs = (grad_local + spread.astype(jnp.float32)).astype(jnp.bfloat16)
    return (outputs, grad_inputs, grad_real, grad_imag)


def solution(mesh):
    placed = (
        P(("len", "pipe"), None, None),
        P(("len", "pipe"), None, None),
        P(),
        P(),
        P("len", None, None),
        P("len", None, None),
        P(),
        P(),
        P(),
        P(),
    )
    return jax.shard_map(
        body,
        mesh=mesh,
        in_specs=placed,
        out_specs=(
            P(("len", "pipe"), None, None),
            P(("len", "pipe"), None, None),
            P("len", None, None),
            P("len", None, None),
        ),
        check_vma=False,
    )
```

```python
import functools
import math

import jax
import jax.numpy as jnp
from jax import lax
from jax.experimental import pallas as pl
from jax.experimental.pallas import tpu as pltpu
from jax.sharding import PartitionSpec as P

COUPLING = 0.125
LINE = 16
CORES = 2
TILE = 256
MESH = pl.DeviceIdType.MESH
BF = jnp.bfloat16
F32 = jnp.float32
GELU_A = math.sqrt(2.0 / math.pi)
GELU_B = GELU_A * 0.044715


def far_first(count):
    return sorted(range(1, count), key=lambda k: (-min(k, count - k), k))


def dot(left, right):
    return jnp.dot(left, right, preferred_element_type=F32)


def dot_nt(left, right):
    return lax.dot_general(left, right, (((1,), (1,)), ((), ())), preferred_element_type=F32)


def dot_tn(left, right):
    return lax.dot_general(left, right, (((0,), (0,)), ((), ())), preferred_element_type=F32)


def turn_cos(index, cell_count):
    half, quarter = cell_count // 2, cell_count // 4
    away = jnp.abs(index - half)
    folded = jnp.minimum(away, half - away)
    x = folded.astype(F32) * (2.0 * math.pi / cell_count)
    y = x * x
    value = jnp.full_like(y, 1.0 / math.factorial(12))
    for power in (10, 8, 6, 4, 2, 0):
        sign = 1.0 if power % 4 == 0 else -1.0
        value = value * y + sign / math.factorial(power)
    return jnp.where(away > quarter, value, -value)


def mode_of(row, line):
    group = row // (2 * line)
    spot = (row // 2) % line
    return ((group // CORES) * line + spot) * CORES + group % CORES


def base_tables(row, col, cell_count, line):
    mode = mode_of(row, line)
    index = mode * col + (cell_count // 4) * (row % 2)
    scale = 1.0 / math.sqrt(cell_count)
    cosine = turn_cos(index % cell_count, cell_count) * scale
    sine = turn_cos((index + 3 * (cell_count // 4)) % cell_count, cell_count) * scale
    return cosine, sine


def shift_factors(row, step, steps, line):
    index = (mode_of(row, line) * step) % steps
    return turn_cos(index, steps), turn_cos((index + 3 * (steps // 4)) % steps, steps)


def kernel_body(
    dims,
    x_hbm, cot_hbm, pw_ref, pb_ref, sr_ref, si_ref, jw_ref, jb_ref, in_ref, out_ref,
    y_hbm, gi_hbm, gr_hbm, gm_hbm,
    xv, cotv, ftab, ttab, pointv, gtv, localv, yv, giv, acc,
    send_g, recv_g, send_z, recv_z,
    own_z, ag_z, own_g, ag_g, ag_x,
    wfull, wsend, wrecv, wtot, grout,
    perm_p, perm_q, sel_f, sel_b, condv, jactv, rowv,
    load_sem, out_sem, ssem, rsem,
):
    line, groups, width, pipes = dims["line"], dims["groups"], dims["width"], dims["pipes"]
    cells, chans, rows = dims["cells"], dims["chans"], dims["rows"]
    chunks = cells // TILE
    len_me, x_me = lax.axis_index("len"), lax.axis_index("pipe")
    c_me = len_me % CORES
    z_me = (len_me // CORES) % line
    y_me = len_me // (CORES * line)
    g_me = y_me * CORES + c_me

    def len_of(group, spot):
        return ((group // CORES) * line + spot) * CORES + group % CORES

    def at_g(k):
        group = (g_me + k) % groups
        return group, {"len": len_of(group, z_me), "pipe": x_me}

    def at_z(k):
        spot = (z_me + k) % line
        return spot, {"len": len_of(g_me, spot), "pipe": x_me}

    def at_x(k):
        column = (x_me + k) % width
        return column, {"len": len_me, "pipe": column}

    peers = {"g": (at_g, groups), "z": (at_z, line), "x": (at_x, width)}

    def send(axis, phase, source, target):
        at, count = peers[axis]
        for k in far_first(count):
            spot, device = at(k)
            pltpu.make_async_remote_copy(
                src_ref=source(spot),
                dst_ref=target,
                send_sem=ssem.at[phase],
                recv_sem=rsem.at[phase],
                device_id=device,
                device_id_type=MESH,
            ).start()

    def drain(sem, phase, blocks, count):
        part = blocks.at[pl.ds(0, count - 1)]
        pltpu.make_async_copy(part, part, sem.at[phase]).wait()

    load_x = pltpu.make_async_copy(x_hbm, xv, load_sem.at[0])
    load_cot = pltpu.make_async_copy(cot_hbm, cotv, load_sem.at[1])
    load_x.start()
    load_cot.start()

    barrier = pltpu.get_barrier_semaphore()
    for at, count in peers.values():
        for k in range(1, count):
            pl.semaphore_signal(barrier, inc=1, device_id=at(k)[1], device_id_type=MESH)

    row_id = lax.broadcasted_iota(jnp.int32, (rows, TILE), 0)
    col_id = lax.broadcasted_iota(jnp.int32, (rows, TILE), 1)
    base_cos, base_sin = base_tables(row_id, col_id, cells, line)
    localv[0:rows, :] = base_cos
    localv[rows : 2 * rows, :] = base_sin
    row_one = lax.broadcasted_iota(jnp.int32, (rows, 1), 0)
    acc[...] = jnp.zeros_like(acc)
    load_x.wait()

    def spectra_step(k, carry):
        turn_c, turn_s = shift_factors(row_one, k, chunks, line)
        table = (localv[0:rows, :] * turn_c - localv[rows : 2 * rows, :] * turn_s).astype(BF)
        ftab[k] = table
        acc[...] += dot(table, xv[pl.ds(k * TILE, TILE), :])
        return carry

    lax.fori_loop(0, chunks, spectra_step, 0)
    send_g[0] = acc[...].astype(BF).reshape(groups, 2 * line, chans)
    pl.semaphore_wait(barrier, (groups - 1) + (line - 1) + (width - 1))

    def hop_g(phase, slot):
        recv_g[slot, g_me] = send_g[slot, g_me]
        send("g", phase, lambda spot: send_g.at[slot, spot], recv_g.at[slot, g_me])

    def hop_z(phase, slot):
        recv_z[slot, z_me] = send_z[slot, z_me]
        send("z", phase, lambda spot: send_z.at[slot, spot], recv_z.at[slot, z_me])

    def to_line(slot):
        block = dot(perm_p[...], recv_g[slot].reshape(rows, chans)).astype(BF)
        send_z[slot] = block.reshape(line, 2 * groups, chans)

    def to_group(slot):
        block = dot_tn(perm_p[...], recv_z[slot].reshape(rows, chans)).astype(BF)
        send_g[slot] = block.reshape(groups, 2 * line, chans)

    hop_g(0, 0)

    def gather_z(phase, slot, first, second):
        part = lax.broadcasted_iota(jnp.int32, (2, chans), 0)
        own_z[slot] = jnp.where(part == 0, first, second).astype(BF)
        ag_z[slot, z_me] = own_z[slot]
        send("z", phase, lambda spot: own_z.at[slot], ag_z.at[slot, z_me])

    def gather_g(phase, slot):
        for spot in range(line):
            rowv[2 * spot : 2 * spot + 2, :] = ag_z[slot, spot].astype(F32)
        own_g[slot] = rowv[...].astype(BF)
        ag_g[slot, g_me] = own_g[slot]
        send("g", phase, lambda spot: own_g.at[slot], ag_g.at[slot, g_me])

    def gather_x(phase, slot):
        ag_x[slot, x_me] = ag_g[slot]
        send("x", phase, lambda spot: ag_g.at[slot], ag_x.at[slot, x_me])

    first_row = xv[0:16, :].astype(F32)[0:1, :]
    last_row = xv[cells - 16 : cells, :].astype(F32)[15:16, :]
    gather_z(1, 0, first_row, last_row)

    to_row = lax.broadcasted_iota(jnp.int32, (rows, rows), 0)
    from_row = lax.broadcasted_iota(jnp.int32, (rows, rows), 1)
    spot_of, group_of = to_row // (2 * groups), (to_row // 2) % groups
    wanted = group_of * (2 * line) + spot_of * 2 + to_row % 2
    perm_p[...] = (from_row == wanted).astype(F32).astype(BF)
    swapped = jnp.where(to_row % 2 == 0, to_row + 1, to_row - 1)
    sign = jnp.where(to_row % 2 == 0, -1.0, 1.0)
    perm_q[...] = jnp.where(from_row == swapped, sign, 0.0).astype(BF)

    drain(rsem, 0, recv_g.at[0], groups)
    to_line(0)
    hop_z(2, 0)

    ids_in, ids_out = in_ref[...].astype(F32), out_ref[...].astype(F32)
    place = lax.broadcasted_iota(jnp.int32, (1, pipes), 1)
    here = place == len_me * width + x_me
    mine_in = jnp.sum(jnp.where(here, ids_in, 0.0), axis=1, keepdims=True)
    mine_out = jnp.sum(jnp.where(here, ids_out, 0.0), axis=1, keepdims=True)
    which = lax.broadcasted_iota(jnp.int32, (8, pipes), 0)

    def matches(ids):
        pair = jnp.where(which == 0, (ids == mine_in).astype(F32), (ids == mine_out).astype(F32))
        return jnp.where(which < 2, pair, 0.0).astype(BF)

    pipe_row = lax.broadcasted_iota(jnp.int32, (pipes, 2 * pipes), 0)
    entry = lax.broadcasted_iota(jnp.int32, (1, 2 * pipes), 1)
    part = entry % 2
    spot_e = (entry // 2) % line
    group_e = (entry // (2 * line)) % groups
    column_e = entry // (2 * line * groups)
    pipe_e = len_of(group_e, spot_e) * width + column_e
    hot_first = jnp.where(pipe_row == jnp.where(part == 0, pipe_e, -1), 1.0, 0.0).astype(BF)
    hot_last = jnp.where(pipe_row == jnp.where(part == 1, pipe_e, -1), 1.0, 0.0).astype(BF)
    match_in, match_out = matches(ids_in), matches(ids_out)
    sel_f[...] = (dot(match_in, hot_first) + dot(match_out, hot_last)).astype(BF)
    both = (match_in.astype(F32) + match_out.astype(F32)).astype(BF)
    sel_b[...] = (dot(both, hot_first) + dot(both, hot_last)).astype(BF)

    drain(rsem, 1, ag_z.at[0], line)
    gather_g(3, 0)

    def point_step(k, carry):
        part_rows = pl.ds(k * TILE, TILE)
        pointv[part_rows, :] = dot(xv[part_rows, :], pw_ref[...]) + pb_ref[...]
        return carry

    lax.fori_loop(0, chunks, point_step, 0)

    drain(rsem, 3, ag_g.at[0], groups)
    gather_x(4, 0)

    drain(rsem, 2, recv_z.at[0], line)
    data = recv_z[0].reshape(rows, chans)
    turned = dot(perm_q[...], data).astype(BF)
    mixed = dot(data, sr_ref[...]) + dot(turned, si_ref[...])
    send_z[1] = mixed.astype(BF).reshape(line, 2 * groups, chans)
    hop_z(5, 1)

    cell_id = lax.broadcasted_iota(jnp.int32, (TILE, rows), 0)
    mode_id = lax.broadcasted_iota(jnp.int32, (TILE, rows), 1)
    side_cos, side_sin = base_tables(mode_id, cell_id, cells, line)
    localv[0:TILE, :] = side_cos
    localv[TILE : 2 * TILE, :] = side_sin
    col_one = lax.broadcasted_iota(jnp.int32, (1, rows), 1)

    def side_step(k, carry):
        turn_c, turn_s = shift_factors(col_one, k, chunks, line)
        ttab[k] = (localv[0:TILE, :] * turn_c - localv[TILE : 2 * TILE, :] * turn_s).astype(BF)
        return carry

    lax.fori_loop(0, chunks, side_step, 0)

    drain(rsem, 4, ag_x.at[0], width)
    sums = dot(sel_f[...], ag_x[0].reshape(2 * pipes, chans))
    junc_act = dot(sums.astype(BF), jw_ref[...]) + jb_ref[...]
    jactv[...] = junc_act
    junc_rows = (junc_act * jax.nn.sigmoid(junc_act)).astype(BF).astype(F32)
    condv[...] = COUPLING * (junc_rows[0:1, :] + junc_rows[1:2, :])

    drain(rsem, 5, recv_z.at[1], line)
    to_group(1)
    hop_g(6, 1)
    weight_row = lax.broadcasted_iota(jnp.int32, (rows, 1), 0)
    doubled = jnp.where(mode_of(weight_row, line) == 0, 1.0, 2.0)
    load_cot.wait()
    drain(rsem, 6, recv_g.at[1], groups)
    scaled = (recv_g[1].reshape(rows, chans).astype(F32) * doubled).astype(BF)
    send_g[2] = scaled.reshape(groups, 2 * line, chans)

    acc[...] = jnp.zeros_like(acc)

    def gelu_step(k, total):
        part_rows = pl.ds(k * TILE, TILE)
        spectral = dot(ttab[k], send_g[2].reshape(rows, chans))
        pre = (spectral + condv[...]).astype(BF).astype(F32)
        s = pointv[part_rows, :] + pre
        square = s * s
        bent = jnp.tanh(s * (GELU_A + GELU_B * square))
        half = 0.5 + 0.5 * bent
        yv[part_rows, :] = (s * half).astype(BF)
        slope = half + (0.5 * s) * (1.0 - bent * bent) * (GELU_A + (3.0 * GELU_B) * square)
        grad = (cotv[part_rows, :].astype(F32) * slope).astype(BF)
        gtv[part_rows, :] = grad
        acc[...] += dot(ftab[k], grad)
        pltpu.make_async_copy(yv.at[part_rows], y_hbm.at[part_rows], out_sem.at[0]).start()
        return total + jnp.sum(grad.astype(F32), axis=0, keepdims=True)

    grad_cond = lax.fori_loop(0, chunks, gelu_step, jnp.zeros((1, chans), F32))
    send_g[3] = (acc[...] * doubled).astype(BF).reshape(groups, 2 * line, chans)
    hop_g(7, 3)
    high = grad_cond.astype(BF).astype(F32)
    gather_z(8, 1, high, grad_cond - high)

    drain(rsem, 7, recv_g.at[3], groups)
    to_line(3)
    hop_z(9, 3)

    drain(rsem, 8, ag_z.at[1], line)
    gather_g(10, 1)

    def local_step(k, carry):
        part_rows = pl.ds(k * TILE, TILE)
        localv[part_rows, :] = dot_nt(gtv[part_rows, :], pw_ref[...])
        return carry

    lax.fori_loop(0, chunks, local_step, 0)
    drain(rsem, 10, ag_g.at[1], groups)
    gather_x(11, 1)

    drain(rsem, 9, recv_z.at[3], line)
    grads = recv_z[3].reshape(rows, chans)
    flipped = dot_tn(perm_q[...], grads).astype(BF)
    back = dot_nt(grads, sr_ref[...]) + dot_nt(flipped, si_ref[...])
    send_z[2] = back.astype(BF).reshape(line, 2 * groups, chans)
    hop_z(12, 2)

    data = recv_z[0].reshape(rows, chans)
    real = dot_tn(data, grads)
    imag = dot_tn(data, flipped)
    share = chans // width
    for column in range(width):
        cut = slice(column * share, (column + 1) * share)
        wfull[column, 0] = real[cut, :]
        wfull[column, 1] = imag[cut, :]
    wsend[...] = wfull[...].astype(BF)
    send("x", 13, lambda spot: wsend.at[spot], wrecv.at[x_me])

    drain(rsem, 11, ag_x.at[1], width)
    junc_grad = COUPLING * dot(sel_b[...], ag_x[1].reshape(2 * pipes, chans))
    junc_act = jactv[...]
    gate = jax.nn.sigmoid(junc_act)
    act_grad = (junc_grad * (gate * (1.0 + junc_act * (1.0 - gate)))).astype(BF)
    jactv[...] = dot_nt(act_grad, jw_ref[...]).astype(BF).astype(F32)

    drain(rsem, 13, wrecv, width)
    wrecv[x_me] = jnp.zeros(wrecv.shape[1:], BF)
    total = wfull[x_me]
    for column in range(width):
        total = total + wrecv[column].astype(F32)
    wtot[x_me] = total.astype(BF)
    send("x", 14, lambda spot: wtot.at[x_me], wtot.at[x_me])

    drain(rsem, 12, recv_z.at[2], line)
    to_group(2)
    hop_g(15, 2)

    drain(rsem, 14, wtot, width)
    for column in range(width):
        cut = slice(column * share, (column + 1) * share)
        grout[0, cut, :] = wtot[column, 0].astype(F32)
        grout[1, cut, :] = wtot[column, 1].astype(F32)
    put_real = pltpu.make_async_copy(grout.at[0], gr_hbm, out_sem.at[1])
    put_imag = pltpu.make_async_copy(grout.at[1], gm_hbm, out_sem.at[2])
    put_real.start()
    put_imag.start()

    drain(rsem, 15, recv_g.at[2], groups)

    def final_step(k, ends):
        part_rows = pl.ds(k * TILE, TILE)
        spread = dot(ttab[k], recv_g[2].reshape(rows, chans))
        if ends is not None:
            spread = spread + ends
        giv[part_rows, :] = (localv[part_rows, :] + spread.astype(BF).astype(F32)).astype(BF)
        pltpu.make_async_copy(giv.at[part_rows], gi_hbm.at[part_rows], out_sem.at[3]).start()

    tile_row = lax.broadcasted_iota(jnp.int32, (TILE, chans), 0)
    final_step(0, jnp.where(tile_row == 0, jactv[0:1, :], 0.0))

    def final_loop(k, carry):
        final_step(k, None)
        return carry

    lax.fori_loop(1, chunks - 1, final_loop, 0)
    final_step(chunks - 1, jnp.where(tile_row == TILE - 1, jactv[1:2, :], 0.0))

    for phase, blocks, count in (
        (0, recv_g.at[0], groups), (1, ag_z.at[0], line), (2, recv_z.at[0], line),
        (3, ag_g.at[0], groups), (4, ag_x.at[0], width), (5, recv_z.at[1], line),
        (6, recv_g.at[1], groups), (7, recv_g.at[3], groups), (8, ag_z.at[1], line),
        (9, recv_z.at[3], line), (10, ag_g.at[1], groups), (11, ag_x.at[1], width),
        (12, recv_z.at[2], line), (13, wrecv, width), (14, wtot, width),
        (15, recv_g.at[2], groups),
    ):
        drain(ssem, phase, blocks, count)
    pltpu.make_async_copy(yv, y_hbm, out_sem.at[0]).wait()
    put_real.wait()
    put_imag.wait()
    pltpu.make_async_copy(giv, gi_hbm, out_sem.at[3]).wait()


def body(
    inputs, cotangent, point_weight, point_bias, spec_real, spec_imag,
    junc_weight, junc_bias, inlet_ids, outlet_ids,
):
    per_dev, cells, chans = inputs.shape
    len_count, width = lax.axis_size("len"), lax.axis_size("pipe")
    line, groups = LINE, len_count // LINE
    rows, pipes = 2 * len_count, inlet_ids.shape[0]
    dims = dict(
        line=line, groups=groups, width=width, pipes=pipes, cells=cells, chans=chans, rows=rows
    )
    share = chans // width
    vm = pltpu.VMEM
    anywhere = pl.BlockSpec(memory_space=pl.ANY)
    inside = pl.BlockSpec(memory_space=pltpu.VMEM)
    y, gi, gr, gm = pl.pallas_call(
        functools.partial(kernel_body, dims),
        out_shape=(
            jax.ShapeDtypeStruct((cells, chans), BF),
            jax.ShapeDtypeStruct((cells, chans), BF),
            jax.ShapeDtypeStruct((chans, chans), F32),
            jax.ShapeDtypeStruct((chans, chans), F32),
        ),
        in_specs=[anywhere] * 2 + [inside] * 8,
        out_specs=(anywhere,) * 4,
        scratch_shapes=[
            vm((cells, chans), BF), vm((cells, chans), BF),
            vm((cells // TILE, rows, TILE), BF), vm((cells // TILE, TILE, rows), BF),
            vm((cells, chans), F32), vm((cells, chans), BF), vm((cells, chans), F32),
            vm((cells, chans), BF), vm((cells, chans), BF), vm((rows, chans), F32),
            vm((4, groups, 2 * line, chans), BF), vm((4, groups, 2 * line, chans), BF),
            vm((4, line, 2 * groups, chans), BF), vm((4, line, 2 * groups, chans), BF),
            vm((2, 2, chans), BF), vm((2, line, 2, chans), BF),
            vm((2, 2 * line, chans), BF), vm((2, groups, 2 * line, chans), BF),
            vm((2, width, groups, 2 * line, chans), BF),
            vm((width, 2, share, chans), F32), vm((width, 2, share, chans), BF),
            vm((width, 2, share, chans), BF), vm((width, 2, share, chans), BF),
            vm((2, chans, chans), F32),
            vm((rows, rows), BF), vm((rows, rows), BF),
            vm((8, 2 * pipes), BF), vm((8, 2 * pipes), BF),
            vm((1, chans), F32), vm((8, chans), F32), vm((2 * line, chans), F32),
            pltpu.SemaphoreType.DMA((2,)), pltpu.SemaphoreType.DMA((4,)),
            pltpu.SemaphoreType.DMA((16,)), pltpu.SemaphoreType.DMA((16,)),
        ],
        compiler_params=pltpu.CompilerParams(
            collective_id=0, has_side_effects=True, vmem_limit_bytes=48 << 20
        ),
        name="operator_step",
    )(
        inputs[0], cotangent[0], point_weight, point_bias[None, :], spec_real[0], spec_imag[0],
        junc_weight, junc_bias[None, :], inlet_ids[None, :], outlet_ids[None, :],
    )
    return y[None], gi[None], gr[None], gm[None]


def solution(mesh):
    split = P(("len", "pipe"), None, None)
    modes = P("len", None, None)
    return jax.shard_map(
        body,
        mesh=mesh,
        in_specs=(split, split, P(), P(), modes, modes, P(), P(), P(), P()),
        out_specs=(split, split, modes, modes),
        check_vma=False,
    )
```

```python
import functools
import math

import jax
import jax.numpy as jnp
from jax import lax
from jax.experimental import pallas as pl
from jax.experimental.pallas import tpu as pltpu
from jax.sharding import PartitionSpec as P

COUPLING = 0.125
LINE = 16
CORES = 2
TILE = 256
MESH = pl.DeviceIdType.MESH
BF = jnp.bfloat16
F32 = jnp.float32
GELU_A = math.sqrt(2.0 / math.pi)
GELU_B = GELU_A * 0.044715


def dot(left, right):
    return jnp.dot(left, right, preferred_element_type=F32)


def dot_nt(left, right):
    return lax.dot_general(left, right, (((1,), (1,)), ((), ())), preferred_element_type=F32)


def dot_tn(left, right):
    return lax.dot_general(left, right, (((0,), (0,)), ((), ())), preferred_element_type=F32)


def turn_cos(index, cell_count):
    half, quarter = cell_count // 2, cell_count // 4
    away = jnp.abs(index - half)
    folded = jnp.minimum(away, half - away)
    x = folded.astype(F32) * (2.0 * math.pi / cell_count)
    y = x * x
    value = jnp.full_like(y, 1.0 / math.factorial(12))
    for power in (10, 8, 6, 4, 2, 0):
        sign = 1.0 if power % 4 == 0 else -1.0
        value = value * y + sign / math.factorial(power)
    return jnp.where(away > quarter, value, -value)


def mode_of(row, chips):
    return (row // 2) % chips * CORES + row // (2 * chips)


def base_tables(row, col, cell_count, chips):
    mode = mode_of(row, chips)
    index = mode * col + (cell_count // 4) * (row % 2)
    scale = 1.0 / math.sqrt(cell_count)
    cosine = turn_cos(index % cell_count, cell_count) * scale
    sine = turn_cos((index + 3 * (cell_count // 4)) % cell_count, cell_count) * scale
    return cosine, sine


def shift_factors(row, step, steps, chips):
    index = (mode_of(row, chips) * step) % steps
    return turn_cos(index, steps), turn_cos((index + 3 * (steps // 4)) % steps, steps)


def kernel_body(
    dims,
    x_hbm, cot_hbm, pw_hbm, pb_hbm, sr_hbm, si_hbm, jw_hbm, jb_hbm, in_hbm, out_hbm,
    y_out, gi_out, gr_out, gm_out,
    xv, cotv, pw_ref, pb_ref, sr_ref, si_ref, jw_ref, jb_ref, in_ref, out_ref,
    ftab, ttab, pointv, gtv, localv, yv, giv, acc,
    stage, duo, data, mixd, back, fin,
    own_z, ag_z, fwd_y, fwd_x, fwd_c, bwd_y, bwd_x, bwd_c,
    wfull, wsend, wrecv, wtot, grout,
    perm_q, sel_f, sel_b, scaledv, condv, jactv, rowv,
    load_sem, out_sem, ssem, rsem,
):
    line, ys, width, pipes = dims["line"], dims["ys"], dims["width"], dims["pipes"]
    cells, chans, rows = dims["cells"], dims["chans"], dims["rows"]
    chips = line * ys
    chunks = cells // TILE
    len_me, x_me = lax.axis_index("len"), lax.axis_index("pipe")
    c_me = len_me % CORES
    chip_me = len_me // CORES
    z_me = chip_me % line
    y_me = chip_me // line
    c_other = 1 - c_me

    def chip_at(dy, dz):
        return (y_me + dy) % ys * line + (z_me + dz) % line

    def on_chip(chip):
        return {"len": chip * CORES + c_me, "pipe": x_me}

    def on_column(k):
        return {"len": len_me, "pipe": (x_me + k) % width}

    sibling = {"len": chip_me * CORES + c_other, "pipe": x_me}
    y_order = sorted(range(ys), key=lambda k: -min(k, ys - k))

    def z_step(j):
        return line // 2 + ((j + 1) // 2) * (1 - 2 * (j % 2))

    def put(phase, source, target, device):
        pltpu.make_async_remote_copy(
            src_ref=source, dst_ref=target, send_sem=ssem.at[phase], recv_sem=rsem.at[phase],
            device_id=device, device_id_type=MESH,
        ).start()

    def drain(sem, phase, part):
        pltpu.make_async_copy(part, part, sem.at[phase]).wait()

    def each_chip(action, low, high):
        def step(j, carry):
            for dy in y_order:
                action(chip_at(dy, z_step(j)))
            return carry

        lax.fori_loop(low, min(high, line - 1), step, 0)
        if high == line:
            for dy in y_order[:-1]:
                action(chip_at(dy, 0))

    loads = [
        pltpu.make_async_copy(source, target, load_sem.at[i])
        for i, (source, target) in enumerate((
            (x_hbm, xv), (sr_hbm, sr_ref), (si_hbm, si_ref), (in_hbm, in_ref), (out_hbm, out_ref),
            (pw_hbm, pw_ref), (pb_hbm, pb_ref), (jw_hbm, jw_ref), (jb_hbm, jb_ref), (cot_hbm, cotv),
        ))
    ]
    for load in loads:
        load.start()

    barrier = pltpu.get_barrier_semaphore()

    def greet(device):
        pl.semaphore_signal(barrier, inc=1, device_id=device, device_id_type=MESH)

    each_chip(lambda chip: greet(on_chip(chip)), 0, line)
    for k in range(1, width):
        greet(on_column(k))
    greet(sibling)

    row_id = lax.broadcasted_iota(jnp.int32, (rows, TILE), 0)
    col_id = lax.broadcasted_iota(jnp.int32, (rows, TILE), 1)
    base_cos, base_sin = base_tables(row_id, col_id, cells, chips)
    localv[0:rows, :] = base_cos
    localv[rows : 2 * rows, :] = base_sin
    row_one = lax.broadcasted_iota(jnp.int32, (rows, 1), 0)
    doubled = jnp.where(mode_of(row_one, chips) == 0, 1.0, 2.0)
    acc[...] = jnp.zeros_like(acc)
    loads[0].wait()

    def spectra_step(k, carry):
        turn_c, turn_s = shift_factors(row_one, k, chunks, chips)
        table = (localv[0:rows, :] * turn_c - localv[rows : 2 * rows, :] * turn_s).astype(BF)
        ftab[k] = table
        acc[...] += dot(table, xv[pl.ds(k * TILE, TILE), :])
        return carry

    lax.fori_loop(0, chunks, spectra_step, 0)
    stage[0] = acc[...].astype(BF).reshape(CORES, chips, 2, chans)
    pl.semaphore_wait(barrier, chips - 1 + width - 1 + 1)

    def swap_out(slot, phase):
        put(phase, stage.at[slot, c_other], duo.at[slot, :, c_me], sibling)
        duo[slot, :, c_me] = stage[slot, c_me]

    def chips_out(slot, phase, low, high):
        if low == 0:
            data[slot, chip_me] = duo[slot, chip_me]
        each_chip(
            lambda chip: put(phase, duo.at[slot, chip], data.at[slot, chip_me], on_chip(chip)),
            low, high,
        )

    def chips_back(slot, phase, low, high):
        if low == 0:
            back[slot, chip_me] = mixd[slot, chip_me]
        each_chip(
            lambda chip: put(phase, mixd.at[slot, chip], back.at[slot, chip_me], on_chip(chip)),
            low, high,
        )

    def swap_back(slot, phase):
        put(phase, back.at[slot, :, c_other], fin.at[slot, c_me], sibling)
        fin[slot, c_me] = back[slot, :, c_me]

    others = pl.ds(0, chips - 1)

    def gather_z(slot, phase, first, second):
        part = lax.broadcasted_iota(jnp.int32, (2, chans), 0)
        own_z[slot] = jnp.where(part == 0, first, second).astype(BF)
        ag_z[slot, z_me] = own_z[slot]

        def step(j, carry):
            put(phase, own_z.at[slot], ag_z.at[slot, z_me], on_chip(chip_at(0, z_step(j))))
            return carry

        lax.fori_loop(0, line - 1, step, 0)

    def gather_y(ref, phase, block):
        ref[y_me] = block
        for dy in y_order[:-1]:
            put(phase, ref.at[y_me], ref.at[y_me], on_chip(chip_at(dy, 0)))

    def gather_x(source, ref, phase):
        ref[x_me] = source[...]
        for k in (2, 1, 3):
            put(phase, source, ref.at[x_me], on_column(k))

    swap_out(0, 0)
    first_row = xv[0:16, :].astype(F32)[0:1, :]
    last_row = xv[cells - 16 : cells, :].astype(F32)[15:16, :]
    gather_z(0, 8, first_row, last_row)
    drain(rsem, 0, stage.at[0, 0])
    chips_out(0, 1, 0, line)

    cell_id = lax.broadcasted_iota(jnp.int32, (TILE, rows), 0)
    mode_id = lax.broadcasted_iota(jnp.int32, (TILE, rows), 1)
    side_cos, side_sin = base_tables(mode_id, cell_id, cells, chips)
    localv[0:TILE, :] = side_cos
    localv[TILE : 2 * TILE, :] = side_sin
    col_one = lax.broadcasted_iota(jnp.int32, (1, rows), 1)

    def side_step(k, carry):
        turn_c, turn_s = shift_factors(col_one, k, chunks, chips)
        ttab[k] = (localv[0:TILE, :] * turn_c - localv[TILE : 2 * TILE, :] * turn_s).astype(BF)
        return carry

    lax.fori_loop(0, chunks, side_step, 0)

    to_row = lax.broadcasted_iota(jnp.int32, (rows, rows), 0)
    from_row = lax.broadcasted_iota(jnp.int32, (rows, rows), 1)
    swapped = jnp.where(to_row % 2 == 0, to_row + 1, to_row - 1)
    sign = jnp.where(to_row % 2 == 0, -1.0, 1.0)
    perm_q[...] = jnp.where(from_row == swapped, sign, 0.0).astype(BF)
    for load in loads[1:9]:
        load.wait()

    drain(rsem, 8, ag_z.at[0, pl.ds(0, line - 1)])
    for spot in range(line):
        rowv[2 * spot : 2 * spot + 2, :] = ag_z[0, spot].astype(F32)
    gather_y(fwd_y, 9, rowv[...].astype(BF))

    drain(rsem, 1, data.at[0, others])
    seen = data[0].reshape(rows, chans)
    turned = dot(perm_q[...], seen).astype(BF)
    mixed = dot(seen, sr_ref[...]) + dot(turned, si_ref[...])
    mixd[0] = mixed.astype(BF).reshape(chips, CORES, 2, chans)
    chips_back(0, 2, 0, line)

    drain(rsem, 9, fwd_y.at[pl.ds(0, ys - 1)])
    gather_x(fwd_y, fwd_x, 10)

    ids_in, ids_out = in_ref[...].astype(F32), out_ref[...].astype(F32)
    place = lax.broadcasted_iota(jnp.int32, (1, pipes), 1)
    here = place == len_me * width + x_me
    mine_in = jnp.sum(jnp.where(here, ids_in, 0.0), axis=1, keepdims=True)
    mine_out = jnp.sum(jnp.where(here, ids_out, 0.0), axis=1, keepdims=True)
    which = lax.broadcasted_iota(jnp.int32, (8, pipes), 0)

    def matches(ids):
        pair = jnp.where(which == 0, (ids == mine_in).astype(F32), (ids == mine_out).astype(F32))
        return jnp.where(which < 2, pair, 0.0).astype(BF)

    def pipe_of(index):
        chip = index % chips
        column = (index // chips) % width
        core = jnp.where(index // (chips * width) == 0, c_me, c_other)
        return (chip * CORES + core) * width + column

    match_in, match_out = matches(ids_in), matches(ids_out)
    entry = lax.broadcasted_iota(jnp.int32, (1, 2 * pipes), 1)
    pipe_e = pipe_of(entry // 2)
    pipe_row = lax.broadcasted_iota(jnp.int32, (pipes, 2 * pipes), 0)
    hot_first = jnp.where(pipe_row == jnp.where(entry % 2 == 0, pipe_e, -1), 1.0, 0.0).astype(BF)
    hot_last = jnp.where(pipe_row == jnp.where(entry % 2 == 1, pipe_e, -1), 1.0, 0.0).astype(BF)
    sel_f[...] = (dot(match_in, hot_first) + dot(match_out, hot_last)).astype(BF)
    entry = lax.broadcasted_iota(jnp.int32, (1, pipes), 1)
    pipe_row = lax.broadcasted_iota(jnp.int32, (pipes, pipes), 0)
    hot = jnp.where(pipe_row == pipe_of(entry), 1.0, 0.0).astype(BF)
    sel_b[...] = (dot(match_in, hot) + dot(match_out, hot)).astype(BF)

    def point_step(k, carry):
        part_rows = pl.ds(k * TILE, TILE)
        pointv[part_rows, :] = dot(xv[part_rows, :], pw_ref[...]) + pb_ref[...]
        return carry

    lax.fori_loop(0, chunks, point_step, 0)

    drain(rsem, 10, fwd_x.at[pl.ds(0, width - 1)])
    put(11, fwd_x, fwd_c, sibling)
    drain(rsem, 2, back.at[0, others])
    swap_back(0, 3)

    drain(rsem, 11, fwd_c)
    sums = dot(sel_f[:, 0:pipes], fwd_x[...].reshape(pipes, chans)) + dot(
        sel_f[:, pipes : 2 * pipes], fwd_c[...].reshape(pipes, chans)
    )
    junc_act = dot(sums.astype(BF), jw_ref[...]) + jb_ref[...]
    jactv[...] = junc_act
    junc_rows = (junc_act * jax.nn.sigmoid(junc_act)).astype(BF).astype(F32)
    condv[...] = COUPLING * (junc_rows[0:1, :] + junc_rows[1:2, :])
    loads[9].wait()

    drain(rsem, 3, fin.at[0, 0])
    scaledv[...] = (fin[0].reshape(rows, chans).astype(F32) * doubled).astype(BF)

    acc[...] = jnp.zeros_like(acc)

    def gelu_step(k, total):
        part_rows = pl.ds(k * TILE, TILE)
        spectral = dot(ttab[k], scaledv[...])
        pre = (spectral + condv[...]).astype(BF).astype(F32)
        s = pointv[part_rows, :] + pre
        square = s * s
        half = 0.5 + 0.5 * jnp.tanh(s * (GELU_A + GELU_B * square))
        value = s * half
        yv[part_rows, :] = value.astype(BF)
        slope = half + (value - value * half) * (2.0 * GELU_A + (6.0 * GELU_B) * square)
        grad = (cotv[part_rows, :].astype(F32) * slope).astype(BF)
        gtv[part_rows, :] = grad
        acc[...] += dot(ftab[k], grad)
        return total + jnp.sum(grad.astype(F32), axis=0, keepdims=True)

    grad_cond = lax.fori_loop(0, chunks, gelu_step, jnp.zeros((1, chans), F32))
    stage[1] = (acc[...] * doubled).astype(BF).reshape(CORES, chips, 2, chans)
    swap_out(1, 4)
    high = grad_cond.astype(BF).astype(F32)
    gather_z(1, 12, high, grad_cond - high)
    drain(rsem, 4, stage.at[0, 0])
    chips_out(1, 5, 0, line)
    put_y = pltpu.make_async_copy(yv, y_out, out_sem.at[0])
    put_y.start()

    def local_step(k, carry):
        part_rows = pl.ds(k * TILE, TILE)
        localv[part_rows, :] = dot_nt(gtv[part_rows, :], pw_ref[...])
        return carry

    lax.fori_loop(0, chunks, local_step, 0)

    drain(rsem, 12, ag_z.at[1, pl.ds(0, line - 1)])
    for spot in range(line):
        rowv[spot : spot + 1, :] = jnp.sum(ag_z[1, spot].astype(F32), axis=0, keepdims=True)
    gather_y(bwd_y, 13, rowv[0:line, :].astype(BF))

    drain(rsem, 5, data.at[1, others])
    grads = data[1].reshape(rows, chans)
    flipped = dot_tn(perm_q[...], grads).astype(BF)
    returned = dot_nt(grads, sr_ref[...]) + dot_nt(flipped, si_ref[...])
    mixd[1] = returned.astype(BF).reshape(chips, CORES, 2, chans)
    seen = data[0].reshape(rows, chans)
    real = dot_tn(seen, grads)
    imag = dot_tn(seen, flipped)
    share = chans // width
    for column in range(width):
        cut = slice(column * share, (column + 1) * share)
        wfull[column, 0] = real[cut, :]
        wfull[column, 1] = imag[cut, :]
    wsend[...] = wfull[...].astype(BF)
    for k in (2, 1, 3):
        put(16, wsend.at[(x_me + k) % width], wrecv.at[x_me], on_column(k))
    chips_back(1, 6, 0, line // 2)
    drain(rsem, 13, bwd_y.at[pl.ds(0, ys - 1)])
    gather_x(bwd_y, bwd_x, 14)
    chips_back(1, 6, line // 2, line)

    drain(rsem, 16, wrecv.at[pl.ds(0, width - 1)])
    wrecv[x_me] = jnp.zeros(wrecv.shape[1:], BF)
    total = wfull[x_me]
    for column in range(width):
        total = total + wrecv[column].astype(F32)
    wtot[x_me] = total.astype(BF)
    for k in (2, 1, 3):
        put(17, wtot.at[x_me], wtot.at[x_me], on_column(k))

    drain(rsem, 14, bwd_x.at[pl.ds(0, width - 1)])
    put(15, bwd_x, bwd_c, sibling)
    drain(rsem, 15, bwd_c)
    half_pipes = pipes // 2
    junc_grad = COUPLING * (
        dot(sel_b[:, 0:half_pipes], bwd_x[...].reshape(half_pipes, chans))
        + dot(sel_b[:, half_pipes:pipes], bwd_c[...].reshape(half_pipes, chans))
    )
    junc_act = jactv[...]
    gate = jax.nn.sigmoid(junc_act)
    act_grad = (junc_grad * (gate * (1.0 + junc_act * (1.0 - gate)))).astype(BF)
    jactv[...] = dot_nt(act_grad, jw_ref[...]).astype(BF).astype(F32)

    drain(rsem, 6, back.at[1, others])
    swap_back(1, 7)
    drain(rsem, 7, fin.at[1, 0])

    def final_step(k, ends):
        part_rows = pl.ds(k * TILE, TILE)
        spread = dot(ttab[k], fin[1].reshape(rows, chans))
        if ends is not None:
            spread = spread + ends
        giv[part_rows, :] = (localv[part_rows, :] + spread.astype(BF).astype(F32)).astype(BF)
        pltpu.make_async_copy(giv.at[part_rows], gi_out.at[part_rows], out_sem.at[3]).start()

    tile_row = lax.broadcasted_iota(jnp.int32, (TILE, chans), 0)
    final_step(0, jnp.where(tile_row == 0, jactv[0:1, :], 0.0))

    def final_loop(k, carry):
        final_step(k, None)
        return carry

    lax.fori_loop(1, chunks - 1, final_loop, 0)
    final_step(chunks - 1, jnp.where(tile_row == TILE - 1, jactv[1:2, :], 0.0))

    drain(rsem, 17, wtot.at[pl.ds(0, width - 1)])
    for column in range(width):
        cut = slice(column * share, (column + 1) * share)
        grout[0, cut, :] = wtot[column, 0].astype(F32)
        grout[1, cut, :] = wtot[column, 1].astype(F32)
    put_real = pltpu.make_async_copy(grout.at[0], gr_out, out_sem.at[1])
    put_imag = pltpu.make_async_copy(grout.at[1], gm_out, out_sem.at[2])
    put_real.start()
    put_imag.start()

    for phase, part in (
        (0, stage.at[0, 0]), (1, data.at[0, others]), (2, back.at[0, others]), (3, fin.at[0, 0]),
        (4, stage.at[0, 0]), (5, data.at[1, others]), (6, back.at[1, others]), (7, fin.at[1, 0]),
        (8, ag_z.at[0, pl.ds(0, line - 1)]), (9, fwd_y.at[pl.ds(0, ys - 1)]),
        (10, fwd_x.at[pl.ds(0, width - 1)]), (11, fwd_c),
        (12, ag_z.at[1, pl.ds(0, line - 1)]), (13, bwd_y.at[pl.ds(0, ys - 1)]),
        (14, bwd_x.at[pl.ds(0, width - 1)]), (15, bwd_c),
        (16, wrecv.at[pl.ds(0, width - 1)]), (17, wtot.at[pl.ds(0, width - 1)]),
    ):
        drain(ssem, phase, part)
    put_y.wait()
    put_real.wait()
    put_imag.wait()
    pltpu.make_async_copy(giv, gi_out, out_sem.at[3]).wait()


def deliver(*refs):
    count = (len(refs) - 1) // 2
    copies = [
        pltpu.make_async_copy(refs[i], refs[count + i], refs[-1].at[i]) for i in range(count)
    ]
    for copy in copies:
        copy.start()
    for copy in copies:
        copy.wait()


def body(
    inputs, cotangent, point_weight, point_bias, spec_real, spec_imag,
    junc_weight, junc_bias, inlet_ids, outlet_ids,
):
    per_dev, cells, chans = inputs.shape
    len_count, width = lax.axis_size("len"), lax.axis_size("pipe")
    line, chips = LINE, len_count // CORES
    ys = chips // line
    rows, pipes = 2 * len_count, inlet_ids.shape[0]
    dims = dict(
        line=line, ys=ys, width=width, pipes=pipes, cells=cells, chans=chans, rows=rows
    )
    share = chans // width
    vm = pltpu.VMEM
    far = pl.BlockSpec(memory_space=pltpu.HBM)
    anywhere = pl.BlockSpec(memory_space=pl.ANY)
    results = (
        jax.ShapeDtypeStruct((cells, chans), BF),
        jax.ShapeDtypeStruct((cells, chans), BF),
        jax.ShapeDtypeStruct((chans, chans), F32),
        jax.ShapeDtypeStruct((chans, chans), F32),
    )
    made = pl.pallas_call(
        functools.partial(kernel_body, dims),
        out_shape=results,
        in_specs=[far] * 10,
        out_specs=(anywhere,) * 4,
        scratch_shapes=[
            vm((cells, chans), BF), vm((cells, chans), BF),
            vm((chans, chans), BF), vm((1, chans), F32), vm((chans, chans), BF),
            vm((chans, chans), BF), vm((chans, chans), BF), vm((1, chans), F32),
            vm((1, pipes), jnp.int32), vm((1, pipes), jnp.int32),
            vm((cells // TILE, rows, TILE), BF), vm((cells // TILE, TILE, rows), BF),
            vm((cells, chans), F32), vm((cells, chans), BF), vm((cells, chans), F32),
            vm((cells, chans), BF), vm((cells, chans), BF), vm((rows, chans), F32),
            vm((2, CORES, chips, 2, chans), BF), vm((2, chips, CORES, 2, chans), BF),
            vm((2, chips, CORES, 2, chans), BF), vm((2, chips, CORES, 2, chans), BF),
            vm((2, chips, CORES, 2, chans), BF), vm((2, CORES, chips, 2, chans), BF),
            vm((2, 2, chans), BF), vm((2, line, 2, chans), BF),
            vm((ys, 2 * line, chans), BF), vm((width, ys, 2 * line, chans), BF),
            vm((width, ys, 2 * line, chans), BF),
            vm((ys, line, chans), BF), vm((width, ys, line, chans), BF),
            vm((width, ys, line, chans), BF),
            vm((width, 2, share, chans), F32), vm((width, 2, share, chans), BF),
            vm((width, 2, share, chans), BF), vm((width, 2, share, chans), BF),
            vm((2, chans, chans), F32),
            vm((rows, rows), BF), vm((8, 2 * pipes), BF), vm((8, pipes), BF),
            vm((rows, chans), BF), vm((1, chans), F32), vm((8, chans), F32),
            vm((2 * line, chans), F32),
            pltpu.SemaphoreType.DMA((10,)), pltpu.SemaphoreType.DMA((4,)),
            pltpu.SemaphoreType.DMA((18,)), pltpu.SemaphoreType.DMA((18,)),
        ],
        compiler_params=pltpu.CompilerParams(
            collective_id=0, has_side_effects=True, vmem_limit_bytes=48 << 20
        ),
        name="operator_step",
    )(*(
        pltpu.with_memory_space_constraint(value, pltpu.HBM)
        for value in (
            inputs[0], cotangent[0], point_weight, point_bias[None, :], spec_real[0],
            spec_imag[0], junc_weight, junc_bias[None, :], inlet_ids[None, :],
            outlet_ids[None, :],
        )
    ))
    y, gi, gr, gm = pl.pallas_call(
        deliver,
        out_shape=results,
        in_specs=[pl.BlockSpec(memory_space=pltpu.VMEM)] * 4,
        out_specs=(far,) * 4,
        scratch_shapes=[pltpu.SemaphoreType.DMA((4,))],
        name="deliver",
    )(*(pltpu.with_memory_space_constraint(value, pltpu.VMEM) for value in made))
    return y[None], gi[None], gr[None], gm[None]


def solution(mesh):
    split = P(("len", "pipe"), None, None)
    modes = P("len", None, None)
    return jax.shard_map(
        body,
        mesh=mesh,
        in_specs=(split, split, P(), P(), modes, modes, P(), P(), P(), P()),
        out_specs=(split, split, modes, modes),
        check_vma=False,
    )
```

```python
import functools
import math

import jax
import jax.numpy as jnp
from jax import lax
from jax.experimental import pallas as pl
from jax.experimental.pallas import tpu as pltpu
from jax.sharding import PartitionSpec as P

COUPLING = 0.125
LINE = 16
CORES = 2
FAR = 5
TILE = 256
MESH = pl.DeviceIdType.MESH
BF = jnp.bfloat16
F32 = jnp.float32
GELU_A = math.sqrt(2.0 / math.pi)
GELU_B = GELU_A * 0.044715


def dot(left, right):
    return jnp.dot(left, right, preferred_element_type=F32)


def dot_nt(left, right):
    return lax.dot_general(left, right, (((1,), (1,)), ((), ())), preferred_element_type=F32)


def dot_tn(left, right):
    return lax.dot_general(left, right, (((0,), (0,)), ((), ())), preferred_element_type=F32)


def turn_cos(index, cell_count):
    half, quarter = cell_count // 2, cell_count // 4
    away = jnp.abs(index - half)
    folded = jnp.minimum(away, half - away)
    x = folded.astype(F32) * (2.0 * math.pi / cell_count)
    y = x * x
    value = jnp.full_like(y, 1.0 / math.factorial(12))
    for power in (10, 8, 6, 4, 2, 0):
        sign = 1.0 if power % 4 == 0 else -1.0
        value = value * y + sign / math.factorial(power)
    return jnp.where(away > quarter, value, -value)


def base_tables(row, col, cell_count):
    index = row // 2 * col + (cell_count // 4) * (row % 2)
    scale = 1.0 / math.sqrt(cell_count)
    cosine = turn_cos(index % cell_count, cell_count) * scale
    sine = turn_cos((index + 3 * (cell_count // 4)) % cell_count, cell_count) * scale
    return cosine, sine


def shift_factors(row, step, steps):
    index = (row // 2 * step) % steps
    return turn_cos(index, steps), turn_cos((index + 3 * (steps // 4)) % steps, steps)


def kernel_body(
    dims,
    x_hbm, cot_hbm, pw_hbm, pb_hbm, sr_hbm, si_hbm, jw_hbm, jb_hbm, in_hbm, out_hbm,
    y_out, gi_out, gr_out, gm_out,
    xv, cotv, pw_ref, pb_ref, sr_ref, si_ref, jw_ref, jb_ref, in_ref, out_ref,
    ftab, ttab, pointv, gtv, localv, yv, giv, acc,
    outbox, duo, inbox,
    own_z, ag_z, fwd_p, fwd_c, bwd_p, bwd_c,
    wfull, wsend, wrecv, wtot, grout,
    perm_q, sel_f, sel_b, scaledv, condv, jactv, rowv,
    load_sem, out_sem, ssem, rsem,
):
    line, ys, width, pipes = dims["line"], dims["ys"], dims["width"], dims["pipes"]
    cells, chans, rows = dims["cells"], dims["chans"], dims["rows"]
    chips = line * ys
    chunks = cells // TILE
    len_me, x_me = lax.axis_index("len"), lax.axis_index("pipe")
    c_me = len_me % CORES
    chip_me = len_me // CORES
    z_me = chip_me % line
    y_me = chip_me // line
    c_other = 1 - c_me

    def chip_at(dy, dz):
        return (y_me + dy) % ys * line + (z_me + dz) % line

    def on_chip(chip, core=None):
        return {"len": chip * CORES + (c_me if core is None else core), "pipe": x_me}

    def on_column(k):
        return {"len": len_me, "pipe": (x_me + k) % width}

    def on_plane(dy, k):
        return {"len": chip_at(dy, 0) * CORES + c_me, "pipe": (x_me + k) % width}

    sibling = {"len": chip_me * CORES + c_other, "pipe": x_me}
    y_order = sorted(range(ys), key=lambda k: -min(k, ys - k))
    x_order = sorted(range(width), key=lambda k: -min(k, width - k))
    plane = [(dy, k) for dy in y_order for k in x_order][:-1]

    def z_step(j):
        return line // 2 + ((j + 1) // 2) * (1 - 2 * (j % 2))

    def put(phase, source, target, device):
        pltpu.make_async_remote_copy(
            src_ref=source, dst_ref=target, send_sem=ssem.at[phase], recv_sem=rsem.at[phase],
            device_id=device, device_id_type=MESH,
        ).start()

    def drain(sem, phase, part):
        pltpu.make_async_copy(part, part, sem.at[phase]).wait()

    def each_chip(action, low, high):
        def step(j, carry):
            for dy in y_order:
                action(chip_at(dy, z_step(j)))
            return carry

        lax.fori_loop(low, min(high, line - 1), step, 0)
        if high == line:
            for dy in y_order[:-1]:
                action(chip_at(dy, 0))

    loads = [
        pltpu.make_async_copy(source, target, load_sem.at[i])
        for i, (source, target) in enumerate((
            (x_hbm, xv), (sr_hbm, sr_ref), (si_hbm, si_ref), (in_hbm, in_ref), (out_hbm, out_ref),
            (pw_hbm, pw_ref), (pb_hbm, pb_ref), (jw_hbm, jw_ref), (jb_hbm, jb_ref), (cot_hbm, cotv),
        ))
    ]
    for load in loads:
        load.start()

    barrier = pltpu.get_barrier_semaphore()

    def greet(device):
        pl.semaphore_signal(barrier, inc=1, device_id=device, device_id_type=MESH)

    def greet_both(chip):
        greet(on_chip(chip))
        greet(on_chip(chip, c_other))

    each_chip(greet_both, 0, FAR)
    each_chip(lambda chip: greet(on_chip(chip)), FAR, line)
    for dy, k in plane:
        if k:
            greet(on_plane(dy, k))
    greet(sibling)

    row_id = lax.broadcasted_iota(jnp.int32, (rows, TILE), 0)
    col_id = lax.broadcasted_iota(jnp.int32, (rows, TILE), 1)
    base_cos, base_sin = base_tables(row_id, col_id, cells)
    localv[0:rows, :] = base_cos
    localv[rows : 2 * rows, :] = base_sin
    row_one = lax.broadcasted_iota(jnp.int32, (rows, 1), 0)
    doubled = jnp.where(row_one < 2, 1.0, 2.0)
    acc[...] = jnp.zeros_like(acc)
    loads[0].wait()

    def spectra_step(k, carry):
        turn_c, turn_s = shift_factors(row_one, k, chunks)
        table = (localv[0:rows, :] * turn_c - localv[rows : 2 * rows, :] * turn_s).astype(BF)
        ftab[k] = table
        acc[...] += dot(table, xv[pl.ds(k * TILE, TILE), :])
        return carry

    lax.fori_loop(0, chunks, spectra_step, 0)
    outbox[0] = acc[...].astype(BF).reshape(chips, CORES, 2, chans)
    pl.semaphore_wait(barrier, chips - 1 + FAR * ys + ys * (width - 1) + 1)

    def exchange(slot):
        phase = 2 * slot
        put(phase, outbox.at[slot, :, c_other], duo.at[slot, :, c_me], sibling)
        duo[slot, :, c_me] = outbox[slot, :, c_me]

        def direct(chip):
            for core in (c_me, c_other):
                put(
                    phase + 1, outbox.at[slot, chip, core], inbox.at[slot, chip_me, c_me],
                    on_chip(chip, core),
                )

        def paired(chip):
            put(phase + 1, duo.at[slot, chip], inbox.at[slot, chip_me], on_chip(chip))

        each_chip(direct, 0, FAR)
        drain(rsem, phase, duo.at[slot, :, 0])
        each_chip(paired, FAR, line)
        inbox[slot, chip_me] = duo[slot, chip_me]

    others = pl.ds(0, chips - 1)

    def gather_z(slot, phase, first, second):
        part = lax.broadcasted_iota(jnp.int32, (2, chans), 0)
        own_z[slot] = jnp.where(part == 0, first, second).astype(BF)
        ag_z[slot, z_me] = own_z[slot]

        def step(j, carry):
            put(phase, own_z.at[slot], ag_z.at[slot, z_me], on_chip(chip_at(0, z_step(j))))
            return carry

        lax.fori_loop(0, line - 1, step, 0)

    def gather_plane(ref, phase, block):
        here = x_me * ys + y_me
        ref[here] = block
        for dy, k in plane:
            put(phase, ref.at[here], ref.at[here], on_plane(dy, k))

    partners = pl.ds(0, len(plane))

    first_row = xv[0:16, :].astype(F32)[0:1, :]
    last_row = xv[cells - 16 : cells, :].astype(F32)[15:16, :]
    gather_z(0, 8, first_row, last_row)
    exchange(0)

    cell_id = lax.broadcasted_iota(jnp.int32, (TILE, rows), 0)
    mode_id = lax.broadcasted_iota(jnp.int32, (TILE, rows), 1)
    side_cos, side_sin = base_tables(mode_id, cell_id, cells)
    localv[0:TILE, :] = side_cos
    localv[TILE : 2 * TILE, :] = side_sin
    col_one = lax.broadcasted_iota(jnp.int32, (1, rows), 1)

    def side_step(k, carry):
        turn_c, turn_s = shift_factors(col_one, k, chunks)
        ttab[k] = (localv[0:TILE, :] * turn_c - localv[TILE : 2 * TILE, :] * turn_s).astype(BF)
        return carry

    lax.fori_loop(0, chunks, side_step, 0)

    to_row = lax.broadcasted_iota(jnp.int32, (rows, rows), 0)
    from_row = lax.broadcasted_iota(jnp.int32, (rows, rows), 1)
    swapped = jnp.where(to_row % 2 == 0, to_row + 1, to_row - 1)
    sign = jnp.where(to_row % 2 == 0, -1.0, 1.0)
    perm_q[...] = jnp.where(from_row == swapped, sign, 0.0).astype(BF)
    for load in loads[1:9]:
        load.wait()

    drain(rsem, 8, ag_z.at[0, pl.ds(0, line - 1)])
    for spot in range(line):
        rowv[2 * spot : 2 * spot + 2, :] = ag_z[0, spot].astype(F32)
    gather_plane(fwd_p, 9, rowv[...].astype(BF))

    drain(rsem, 1, inbox.at[0, others])
    seen = inbox[0].reshape(rows, chans)
    turned = dot(perm_q[...], seen).astype(BF)
    mixed = dot(seen, sr_ref[...]) + dot(turned, si_ref[...])
    outbox[1] = mixed.astype(BF).reshape(chips, CORES, 2, chans)
    exchange(1)
    drain(rsem, 9, fwd_p.at[partners])
    put(10, fwd_p, fwd_c, sibling)

    ids_in, ids_out = in_ref[...].astype(F32), out_ref[...].astype(F32)
    place = lax.broadcasted_iota(jnp.int32, (1, pipes), 1)
    here = place == len_me * width + x_me
    mine_in = jnp.sum(jnp.where(here, ids_in, 0.0), axis=1, keepdims=True)
    mine_out = jnp.sum(jnp.where(here, ids_out, 0.0), axis=1, keepdims=True)
    which = lax.broadcasted_iota(jnp.int32, (8, pipes), 0)

    def matches(ids):
        pair = jnp.where(which == 0, (ids == mine_in).astype(F32), (ids == mine_out).astype(F32))
        return jnp.where(which < 2, pair, 0.0).astype(BF)

    def pipe_of(index):
        chip = index % chips
        column = (index // chips) % width
        core = jnp.where(index // (chips * width) == 0, c_me, c_other)
        return (chip * CORES + core) * width + column

    match_in, match_out = matches(ids_in), matches(ids_out)
    entry = lax.broadcasted_iota(jnp.int32, (1, 2 * pipes), 1)
    pipe_e = pipe_of(entry // 2)
    pipe_row = lax.broadcasted_iota(jnp.int32, (pipes, 2 * pipes), 0)
    hot_first = jnp.where(pipe_row == jnp.where(entry % 2 == 0, pipe_e, -1), 1.0, 0.0).astype(BF)
    hot_last = jnp.where(pipe_row == jnp.where(entry % 2 == 1, pipe_e, -1), 1.0, 0.0).astype(BF)
    sel_f[...] = (dot(match_in, hot_first) + dot(match_out, hot_last)).astype(BF)
    entry = lax.broadcasted_iota(jnp.int32, (1, pipes), 1)
    pipe_row = lax.broadcasted_iota(jnp.int32, (pipes, pipes), 0)
    hot = jnp.where(pipe_row == pipe_of(entry), 1.0, 0.0).astype(BF)
    sel_b[...] = (dot(match_in, hot) + dot(match_out, hot)).astype(BF)

    def point_step(k, carry):
        part_rows = pl.ds(k * TILE, TILE)
        pointv[part_rows, :] = dot(xv[part_rows, :], pw_ref[...]) + pb_ref[...]
        return carry

    lax.fori_loop(0, chunks, point_step, 0)

    drain(rsem, 10, fwd_c)
    sums = dot(sel_f[:, 0:pipes], fwd_p[...].reshape(pipes, chans)) + dot(
        sel_f[:, pipes : 2 * pipes], fwd_c[...].reshape(pipes, chans)
    )
    junc_act = dot(sums.astype(BF), jw_ref[...]) + jb_ref[...]
    jactv[...] = junc_act
    junc_rows = (junc_act * jax.nn.sigmoid(junc_act)).astype(BF).astype(F32)
    condv[...] = COUPLING * (junc_rows[0:1, :] + junc_rows[1:2, :])
    loads[9].wait()

    drain(rsem, 3, inbox.at[1, others])
    scaledv[...] = (inbox[1].reshape(rows, chans).astype(F32) * doubled).astype(BF)

    acc[...] = jnp.zeros_like(acc)

    def gelu_step(k, total):
        part_rows = pl.ds(k * TILE, TILE)
        spectral = dot(ttab[k], scaledv[...])
        pre = (spectral + condv[...]).astype(BF).astype(F32)
        s = pointv[part_rows, :] + pre
        square = s * s
        half = 0.5 + 0.5 * jnp.tanh(s * (GELU_A + GELU_B * square))
        value = s * half
        yv[part_rows, :] = value.astype(BF)
        slope = half + (value - value * half) * (2.0 * GELU_A + (6.0 * GELU_B) * square)
        grad = (cotv[part_rows, :].astype(F32) * slope).astype(BF)
        gtv[part_rows, :] = grad
        acc[...] += dot(ftab[k], grad)
        return total + jnp.sum(grad.astype(F32), axis=0, keepdims=True)

    grad_cond = lax.fori_loop(0, chunks, gelu_step, jnp.zeros((1, chans), F32), unroll=True)
    outbox[2] = (acc[...] * doubled).astype(BF).reshape(chips, CORES, 2, chans)
    high = grad_cond.astype(BF).astype(F32)
    gather_z(1, 11, high, grad_cond - high)
    exchange(2)
    put_y = pltpu.make_async_copy(yv, y_out, out_sem.at[0])
    put_y.start()

    def local_step(k, carry):
        part_rows = pl.ds(k * TILE, TILE)
        localv[part_rows, :] = dot_nt(gtv[part_rows, :], pw_ref[...])
        return carry

    lax.fori_loop(0, chunks, local_step, 0)

    drain(rsem, 11, ag_z.at[1, pl.ds(0, line - 1)])
    for spot in range(line):
        rowv[spot : spot + 1, :] = jnp.sum(ag_z[1, spot].astype(F32), axis=0, keepdims=True)
    gather_plane(bwd_p, 12, rowv[0:line, :].astype(BF))

    drain(rsem, 5, inbox.at[2, others])
    grads = inbox[2].reshape(rows, chans)
    flipped = dot_tn(perm_q[...], grads).astype(BF)
    returned = dot_nt(grads, sr_ref[...]) + dot_nt(flipped, si_ref[...])
    outbox[3] = returned.astype(BF).reshape(chips, CORES, 2, chans)
    seen = inbox[0].reshape(rows, chans)
    real = dot_tn(seen, grads)
    imag = dot_tn(seen, flipped)
    share = chans // width
    for column in range(width):
        cut = slice(column * share, (column + 1) * share)
        wfull[column, 0] = real[cut, :]
        wfull[column, 1] = imag[cut, :]
    wsend[...] = wfull[...].astype(BF)
    for k in x_order[:-1]:
        put(14, wsend.at[(x_me + k) % width], wrecv.at[x_me], on_column(k))
    exchange(3)
    drain(rsem, 12, bwd_p.at[partners])
    put(13, bwd_p, bwd_c, sibling)

    drain(rsem, 14, wrecv.at[pl.ds(0, width - 1)])
    wrecv[x_me] = jnp.zeros(wrecv.shape[1:], BF)
    total = wfull[x_me]
    for column in range(width):
        total = total + wrecv[column].astype(F32)
    wtot[x_me] = total.astype(BF)
    for k in x_order[:-1]:
        put(15, wtot.at[x_me], wtot.at[x_me], on_column(k))

    drain(rsem, 13, bwd_c)
    half_pipes = pipes // 2
    junc_grad = COUPLING * (
        dot(sel_b[:, 0:half_pipes], bwd_p[...].reshape(half_pipes, chans))
        + dot(sel_b[:, half_pipes:pipes], bwd_c[...].reshape(half_pipes, chans))
    )
    junc_act = jactv[...]
    gate = jax.nn.sigmoid(junc_act)
    act_grad = (junc_grad * (gate * (1.0 + junc_act * (1.0 - gate)))).astype(BF)
    jactv[...] = dot_nt(act_grad, jw_ref[...]).astype(BF).astype(F32)

    drain(rsem, 7, inbox.at[3, others])

    def final_step(k, ends):
        part_rows = pl.ds(k * TILE, TILE)
        spread = dot(ttab[k], inbox[3].reshape(rows, chans))
        if ends is not None:
            spread = spread + ends
        giv[part_rows, :] = (localv[part_rows, :] + spread.astype(BF).astype(F32)).astype(BF)
        pltpu.make_async_copy(giv.at[part_rows], gi_out.at[part_rows], out_sem.at[3]).start()

    tile_row = lax.broadcasted_iota(jnp.int32, (TILE, chans), 0)
    final_step(0, jnp.where(tile_row == 0, jactv[0:1, :], 0.0))

    def final_loop(k, carry):
        final_step(k, None)
        return carry

    lax.fori_loop(1, chunks - 1, final_loop, 0, unroll=True)
    final_step(chunks - 1, jnp.where(tile_row == TILE - 1, jactv[1:2, :], 0.0))

    drain(rsem, 15, wtot.at[pl.ds(0, width - 1)])
    for column in range(width):
        cut = slice(column * share, (column + 1) * share)
        grout[0, cut, :] = wtot[column, 0].astype(F32)
        grout[1, cut, :] = wtot[column, 1].astype(F32)
    put_real = pltpu.make_async_copy(grout.at[0], gr_out, out_sem.at[1])
    put_imag = pltpu.make_async_copy(grout.at[1], gm_out, out_sem.at[2])
    put_real.start()
    put_imag.start()

    for slot in range(4):
        drain(ssem, 2 * slot, duo.at[slot, :, 0])
        drain(ssem, 2 * slot + 1, inbox.at[slot, others])
    for phase, part in (
        (8, ag_z.at[0, pl.ds(0, line - 1)]),
        (9, fwd_p.at[partners]), (10, fwd_c),
        (11, ag_z.at[1, pl.ds(0, line - 1)]),
        (12, bwd_p.at[partners]), (13, bwd_c),
        (14, wrecv.at[pl.ds(0, width - 1)]), (15, wtot.at[pl.ds(0, width - 1)]),
    ):
        drain(ssem, phase, part)
    put_y.wait()
    put_real.wait()
    put_imag.wait()
    pltpu.make_async_copy(giv, gi_out, out_sem.at[3]).wait()


def deliver(*refs):
    count = (len(refs) - 1) // 2
    copies = [
        pltpu.make_async_copy(refs[i], refs[count + i], refs[-1].at[i]) for i in range(count)
    ]
    for copy in copies:
        copy.start()
    for copy in copies:
        copy.wait()


def body(
    inputs, cotangent, point_weight, point_bias, spec_real, spec_imag,
    junc_weight, junc_bias, inlet_ids, outlet_ids,
):
    per_dev, cells, chans = inputs.shape
    len_count, width = lax.axis_size("len"), lax.axis_size("pipe")
    line, chips = LINE, len_count // CORES
    ys = chips // line
    rows, pipes = 2 * len_count, inlet_ids.shape[0]
    dims = dict(
        line=line, ys=ys, width=width, pipes=pipes, cells=cells, chans=chans, rows=rows
    )
    share = chans // width
    vm = pltpu.VMEM
    far = pl.BlockSpec(memory_space=pltpu.HBM)
    anywhere = pl.BlockSpec(memory_space=pl.ANY)
    results = (
        jax.ShapeDtypeStruct((cells, chans), BF),
        jax.ShapeDtypeStruct((cells, chans), BF),
        jax.ShapeDtypeStruct((chans, chans), F32),
        jax.ShapeDtypeStruct((chans, chans), F32),
    )
    made = pl.pallas_call(
        functools.partial(kernel_body, dims),
        out_shape=results,
        in_specs=[far] * 10,
        out_specs=(anywhere,) * 4,
        scratch_shapes=[
            vm((cells, chans), BF), vm((cells, chans), BF),
            vm((chans, chans), BF), vm((1, chans), F32), vm((chans, chans), BF),
            vm((chans, chans), BF), vm((chans, chans), BF), vm((1, chans), F32),
            vm((1, pipes), jnp.int32), vm((1, pipes), jnp.int32),
            vm((cells // TILE, rows, TILE), BF), vm((cells // TILE, TILE, rows), BF),
            vm((cells, chans), F32), vm((cells, chans), BF), vm((cells, chans), F32),
            vm((cells, chans), BF), vm((cells, chans), BF), vm((rows, chans), F32),
            vm((4, chips, CORES, 2, chans), BF), vm((4, chips, CORES, 2, chans), BF),
            vm((4, chips, CORES, 2, chans), BF),
            vm((2, 2, chans), BF), vm((2, line, 2, chans), BF),
            vm((width * ys, 2 * line, chans), BF), vm((width * ys, 2 * line, chans), BF),
            vm((width * ys, line, chans), BF), vm((width * ys, line, chans), BF),
            vm((width, 2, share, chans), F32), vm((width, 2, share, chans), BF),
            vm((width, 2, share, chans), BF), vm((width, 2, share, chans), BF),
            vm((2, chans, chans), F32),
            vm((rows, rows), BF), vm((8, 2 * pipes), BF), vm((8, pipes), BF),
            vm((rows, chans), BF), vm((1, chans), F32), vm((8, chans), F32),
            vm((2 * line, chans), F32),
            pltpu.SemaphoreType.DMA((10,)), pltpu.SemaphoreType.DMA((4,)),
            pltpu.SemaphoreType.DMA((16,)), pltpu.SemaphoreType.DMA((16,)),
        ],
        compiler_params=pltpu.CompilerParams(
            collective_id=0, has_side_effects=True, vmem_limit_bytes=48 << 20
        ),
        name="operator_step",
    )(*(
        pltpu.with_memory_space_constraint(value, pltpu.HBM)
        for value in (
            inputs[0], cotangent[0], point_weight, point_bias[None, :], spec_real[0],
            spec_imag[0], junc_weight, junc_bias[None, :], inlet_ids[None, :],
            outlet_ids[None, :],
        )
    ))
    y, gi, gr, gm = pl.pallas_call(
        deliver,
        out_shape=results,
        in_specs=[pl.BlockSpec(memory_space=pltpu.VMEM)] * 4,
        out_specs=(far,) * 4,
        scratch_shapes=[pltpu.SemaphoreType.DMA((4,))],
        name="deliver",
    )(*(pltpu.with_memory_space_constraint(value, pltpu.VMEM) for value in made))
    return y[None], gi[None], gr[None], gm[None]


def solution(mesh):
    split = P(("len", "pipe"), None, None)
    modes = P("len", None, None)
    return jax.shard_map(
        body,
        mesh=mesh,
        in_specs=(split, split, P(), P(), modes, modes, P(), P(), P(), P()),
        out_specs=(split, split, modes, modes),
        check_vma=False,
    )
```

```python
import functools
import math

import jax
import jax.numpy as jnp
from jax import lax
from jax.experimental import pallas as pl
from jax.experimental.pallas import tpu as pltpu
from jax.sharding import PartitionSpec as P

COUPLING = 0.125
LINE = 16
CORES = 2
FAR = 5
TILE = 256
MESH = pl.DeviceIdType.MESH
BF = jnp.bfloat16
F32 = jnp.float32
GELU_A = math.sqrt(2.0 / math.pi)
GELU_B = GELU_A * 0.044715


def dot(left, right):
    return jnp.dot(left, right, preferred_element_type=F32)


def dot_nt(left, right):
    return lax.dot_general(left, right, (((1,), (1,)), ((), ())), preferred_element_type=F32)


def dot_tn(left, right):
    return lax.dot_general(left, right, (((0,), (0,)), ((), ())), preferred_element_type=F32)


def turn_cos(index, cell_count):
    half, quarter = cell_count // 2, cell_count // 4
    away = jnp.abs(index - half)
    folded = jnp.minimum(away, half - away)
    x = folded.astype(F32) * (2.0 * math.pi / cell_count)
    y = x * x
    value = jnp.full_like(y, 1.0 / math.factorial(12))
    for power in (10, 8, 6, 4, 2, 0):
        sign = 1.0 if power % 4 == 0 else -1.0
        value = value * y + sign / math.factorial(power)
    return jnp.where(away > quarter, value, -value)


def base_tables(row, col, cell_count):
    index = row // 2 * col + (cell_count // 4) * (row % 2)
    scale = 1.0 / math.sqrt(cell_count)
    cosine = turn_cos(index % cell_count, cell_count) * scale
    sine = turn_cos((index + 3 * (cell_count // 4)) % cell_count, cell_count) * scale
    return cosine, sine


def shift_factors(row, step, steps):
    index = (row // 2 * step) % steps
    return turn_cos(index, steps), turn_cos((index + 3 * (steps // 4)) % steps, steps)


def kernel_body(
    dims,
    x_hbm, cot_hbm, pw_hbm, pb_hbm, sr_hbm, si_hbm, jw_hbm, jb_hbm, in_hbm, out_hbm,
    yv, localv, ttab, modes, jactv, grv, gmv,
    xv, cotv, pw_ref, pb_ref, sr_ref, si_ref, jw_ref, jb_ref, in_ref, out_ref,
    ftab, pointv, gtv, acc,
    outbox, duo, inbox,
    own_z, ag_z, fwd_p, fwd_c, bwd_p, bwd_c,
    wfull, wsend, wrecv, wtot,
    perm_q, sel_f, sel_b, scaledv, condv, rowv,
    load_sem, ssem, rsem,
):
    line, ys, width, pipes = dims["line"], dims["ys"], dims["width"], dims["pipes"]
    cells, chans, rows = dims["cells"], dims["chans"], dims["rows"]
    chips = line * ys
    chunks = cells // TILE
    len_me, x_me = lax.axis_index("len"), lax.axis_index("pipe")
    c_me = len_me % CORES
    chip_me = len_me // CORES
    z_me = chip_me % line
    y_me = chip_me // line
    c_other = 1 - c_me

    def chip_at(dy, dz):
        return (y_me + dy) % ys * line + (z_me + dz) % line

    def on_chip(chip, core=None):
        return {"len": chip * CORES + (c_me if core is None else core), "pipe": x_me}

    def on_column(k):
        return {"len": len_me, "pipe": (x_me + k) % width}

    def on_plane(dy, k):
        return {"len": chip_at(dy, 0) * CORES + c_me, "pipe": (x_me + k) % width}

    sibling = {"len": chip_me * CORES + c_other, "pipe": x_me}
    y_order = sorted(range(ys), key=lambda k: -min(k, ys - k))
    x_order = sorted(range(width), key=lambda k: -min(k, width - k))
    plane = [(dy, k) for dy in y_order for k in x_order][:-1]

    def z_step(j):
        return line // 2 + ((j + 1) // 2) * (1 - 2 * (j % 2))

    def put(phase, source, target, device):
        pltpu.make_async_remote_copy(
            src_ref=source, dst_ref=target, send_sem=ssem.at[phase], recv_sem=rsem.at[phase],
            device_id=device, device_id_type=MESH,
        ).start()

    def drain(sem, phase, part):
        pltpu.make_async_copy(part, part, sem.at[phase]).wait()

    def each_chip(action, low, high):
        def step(j, carry):
            for dy in y_order:
                action(chip_at(dy, z_step(j)))
            return carry

        lax.fori_loop(low, min(high, line - 1), step, 0)
        if high == line:
            for dy in y_order[:-1]:
                action(chip_at(dy, 0))

    barrier = pltpu.get_barrier_semaphore()

    def greet(device):
        pl.semaphore_signal(barrier, inc=1, device_id=device, device_id_type=MESH)

    def greet_both(chip):
        greet(on_chip(chip))
        greet(on_chip(chip, c_other))

    each_chip(greet_both, 0, FAR)
    each_chip(lambda chip: greet(on_chip(chip)), FAR, line)
    for dy, k in plane:
        if k:
            greet(on_plane(dy, k))
    greet(sibling)

    loads = [
        pltpu.make_async_copy(source, target, load_sem.at[i])
        for i, (source, target) in enumerate((
            (x_hbm, xv), (sr_hbm, sr_ref), (si_hbm, si_ref), (in_hbm, in_ref), (out_hbm, out_ref),
            (pw_hbm, pw_ref), (pb_hbm, pb_ref), (jw_hbm, jw_ref), (jb_hbm, jb_ref), (cot_hbm, cotv),
        ))
    ]
    for load in loads:
        load.start()

    row_id = lax.broadcasted_iota(jnp.int32, (rows, TILE), 0)
    col_id = lax.broadcasted_iota(jnp.int32, (rows, TILE), 1)
    base_cos, base_sin = base_tables(row_id, col_id, cells)
    localv[0:rows, :] = base_cos
    localv[rows : 2 * rows, :] = base_sin
    row_one = lax.broadcasted_iota(jnp.int32, (rows, 1), 0)
    doubled = jnp.where(row_one < 2, 1.0, 2.0)
    acc[...] = jnp.zeros_like(acc)
    loads[0].wait()

    def spectra_step(k, carry):
        turn_c, turn_s = shift_factors(row_one, k, chunks)
        table = (localv[0:rows, :] * turn_c - localv[rows : 2 * rows, :] * turn_s).astype(BF)
        ftab[k] = table
        acc[...] += dot(table, xv[pl.ds(k * TILE, TILE), :])
        return carry

    lax.fori_loop(0, chunks, spectra_step, 0)
    outbox[0] = acc[...].astype(BF).reshape(chips, CORES, 2, chans)
    cell_id = lax.broadcasted_iota(jnp.int32, (TILE, rows), 0)
    mode_id = lax.broadcasted_iota(jnp.int32, (TILE, rows), 1)
    side_cos, side_sin = base_tables(mode_id, cell_id, cells)
    localv[0:TILE, :] = side_cos
    localv[TILE : 2 * TILE, :] = side_sin
    col_one = lax.broadcasted_iota(jnp.int32, (1, rows), 1)

    def side_step(k, carry):
        turn_c, turn_s = shift_factors(col_one, k, chunks)
        ttab[k] = (localv[0:TILE, :] * turn_c - localv[TILE : 2 * TILE, :] * turn_s).astype(BF)
        return carry

    lax.fori_loop(0, chunks, side_step, 0)

    to_row = lax.broadcasted_iota(jnp.int32, (rows, rows), 0)
    from_row = lax.broadcasted_iota(jnp.int32, (rows, rows), 1)
    swapped = jnp.where(to_row % 2 == 0, to_row + 1, to_row - 1)
    sign = jnp.where(to_row % 2 == 0, -1.0, 1.0)
    perm_q[...] = jnp.where(from_row == swapped, sign, 0.0).astype(BF)
    pl.semaphore_wait(barrier, chips - 1 + FAR * ys + ys * (width - 1) + 1)

    def exchange(slot):
        phase = 2 * slot
        put(phase, outbox.at[slot, :, c_other], duo.at[slot, :, c_me], sibling)
        duo[slot, :, c_me] = outbox[slot, :, c_me]

        def direct(chip):
            for core in (c_me, c_other):
                put(
                    phase + 1, outbox.at[slot, chip, core], inbox.at[slot, chip_me, c_me],
                    on_chip(chip, core),
                )

        def paired(chip):
            put(phase + 1, duo.at[slot, chip], inbox.at[slot, chip_me], on_chip(chip))

        each_chip(direct, 0, FAR)
        drain(rsem, phase, duo.at[slot, :, 0])
        each_chip(paired, FAR, line)
        inbox[slot, chip_me] = duo[slot, chip_me]

    others = pl.ds(0, chips - 1)

    def gather_z(slot, phase, first, second):
        part = lax.broadcasted_iota(jnp.int32, (2, chans), 0)
        own_z[slot] = jnp.where(part == 0, first, second).astype(BF)
        ag_z[slot, z_me] = own_z[slot]

        def step(j, carry):
            put(phase, own_z.at[slot], ag_z.at[slot, z_me], on_chip(chip_at(0, z_step(j))))
            return carry

        lax.fori_loop(0, line - 1, step, 0)

    def gather_plane(ref, phase, block):
        here = x_me * ys + y_me
        ref[here] = block
        for dy, k in plane:
            put(phase, ref.at[here], ref.at[here], on_plane(dy, k))

    partners = pl.ds(0, len(plane))

    first_row = xv[0:16, :].astype(F32)[0:1, :]
    last_row = xv[cells - 16 : cells, :].astype(F32)[15:16, :]
    gather_z(0, 8, first_row, last_row)
    exchange(0)

    for load in loads[1:9]:
        load.wait()

    ids_in, ids_out = in_ref[...].astype(F32), out_ref[...].astype(F32)
    place = lax.broadcasted_iota(jnp.int32, (1, pipes), 1)
    here = place == len_me * width + x_me
    mine_in = jnp.sum(jnp.where(here, ids_in, 0.0), axis=1, keepdims=True)
    mine_out = jnp.sum(jnp.where(here, ids_out, 0.0), axis=1, keepdims=True)
    which = lax.broadcasted_iota(jnp.int32, (8, pipes), 0)

    def matches(ids):
        pair = jnp.where(which == 0, (ids == mine_in).astype(F32), (ids == mine_out).astype(F32))
        return jnp.where(which < 2, pair, 0.0).astype(BF)

    def pipe_of(index):
        chip = index % chips
        column = (index // chips) % width
        core = jnp.where(index // (chips * width) == 0, c_me, c_other)
        return (chip * CORES + core) * width + column

    match_in, match_out = matches(ids_in), matches(ids_out)
    entry = lax.broadcasted_iota(jnp.int32, (1, 2 * pipes), 1)
    pipe_e = pipe_of(entry // 2)
    pipe_row = lax.broadcasted_iota(jnp.int32, (pipes, 2 * pipes), 0)
    hot_first = jnp.where(pipe_row == jnp.where(entry % 2 == 0, pipe_e, -1), 1.0, 0.0).astype(BF)
    hot_last = jnp.where(pipe_row == jnp.where(entry % 2 == 1, pipe_e, -1), 1.0, 0.0).astype(BF)
    sel_f[...] = (dot(match_in, hot_first) + dot(match_out, hot_last)).astype(BF)
    entry = lax.broadcasted_iota(jnp.int32, (1, pipes), 1)
    pipe_row = lax.broadcasted_iota(jnp.int32, (pipes, pipes), 0)
    hot = jnp.where(pipe_row == pipe_of(entry), 1.0, 0.0).astype(BF)
    sel_b[...] = (dot(match_in, hot) + dot(match_out, hot)).astype(BF)

    drain(rsem, 8, ag_z.at[0, pl.ds(0, line - 1)])
    for spot in range(line):
        rowv[2 * spot : 2 * spot + 2, :] = ag_z[0, spot].astype(F32)
    gather_plane(fwd_p, 9, rowv[...].astype(BF))

    drain(rsem, 1, inbox.at[0, others])
    seen = inbox[0].reshape(rows, chans)
    turned = dot(perm_q[...], seen).astype(BF)
    mixed = dot(seen, sr_ref[...]) + dot(turned, si_ref[...])
    outbox[1] = mixed.astype(BF).reshape(chips, CORES, 2, chans)
    exchange(1)
    drain(rsem, 9, fwd_p.at[partners])
    put(10, fwd_p, fwd_c, sibling)

    def point_step(k, carry):
        part_rows = pl.ds(k * TILE, TILE)
        pointv[part_rows, :] = dot(xv[part_rows, :], pw_ref[...]) + pb_ref[...]
        return carry

    lax.fori_loop(0, chunks, point_step, 0)

    drain(rsem, 10, fwd_c)
    sums = dot(sel_f[:, 0:pipes], fwd_p[...].reshape(pipes, chans)) + dot(
        sel_f[:, pipes : 2 * pipes], fwd_c[...].reshape(pipes, chans)
    )
    junc_act = dot(sums.astype(BF), jw_ref[...]) + jb_ref[...]
    jactv[...] = junc_act
    junc_rows = (junc_act * jax.nn.sigmoid(junc_act)).astype(BF).astype(F32)
    condv[...] = COUPLING * (junc_rows[0:1, :] + junc_rows[1:2, :])
    loads[9].wait()

    drain(rsem, 3, inbox.at[1, others])
    scaledv[...] = (inbox[1].reshape(rows, chans).astype(F32) * doubled).astype(BF)

    acc[...] = jnp.zeros_like(acc)

    def gelu_step(k, total):
        part_rows = pl.ds(k * TILE, TILE)
        spectral = dot(ttab[k], scaledv[...])
        pre = (spectral + condv[...]).astype(BF).astype(F32)
        s = pointv[part_rows, :] + pre
        square = s * s
        half = 0.5 + 0.5 * jnp.tanh(s * (GELU_A + GELU_B * square))
        value = s * half
        yv[part_rows, :] = value.astype(BF)
        slope = half + (value - value * half) * (2.0 * GELU_A + (6.0 * GELU_B) * square)
        grad = (cotv[part_rows, :].astype(F32) * slope).astype(BF)
        gtv[part_rows, :] = grad
        acc[...] += dot(ftab[k], grad)
        return total + jnp.sum(grad.astype(F32), axis=0, keepdims=True)

    grad_cond = lax.fori_loop(0, chunks, gelu_step, jnp.zeros((1, chans), F32), unroll=True)
    outbox[2] = (acc[...] * doubled).astype(BF).reshape(chips, CORES, 2, chans)
    high = grad_cond.astype(BF).astype(F32)
    gather_z(1, 11, high, grad_cond - high)
    exchange(2)
    def local_step(k, carry):
        part_rows = pl.ds(k * TILE, TILE)
        localv[part_rows, :] = dot_nt(gtv[part_rows, :], pw_ref[...])
        return carry

    lax.fori_loop(0, chunks, local_step, 0)

    drain(rsem, 11, ag_z.at[1, pl.ds(0, line - 1)])
    for spot in range(line):
        rowv[spot : spot + 1, :] = jnp.sum(ag_z[1, spot].astype(F32), axis=0, keepdims=True)
    gather_plane(bwd_p, 12, rowv[0:line, :].astype(BF))

    drain(rsem, 5, inbox.at[2, others])
    grads = inbox[2].reshape(rows, chans)
    flipped = dot_tn(perm_q[...], grads).astype(BF)
    returned = dot_nt(grads, sr_ref[...]) + dot_nt(flipped, si_ref[...])
    outbox[3] = returned.astype(BF).reshape(chips, CORES, 2, chans)
    seen = inbox[0].reshape(rows, chans)
    real = dot_tn(seen, grads)
    imag = dot_tn(seen, flipped)
    share = chans // width
    for column in range(width):
        cut = slice(column * share, (column + 1) * share)
        wfull[column, 0] = real[cut, :]
        wfull[column, 1] = imag[cut, :]
    wsend[...] = wfull[...].astype(BF)
    for k in x_order[:-1]:
        put(14, wsend.at[(x_me + k) % width], wrecv.at[x_me], on_column(k))
    exchange(3)
    drain(rsem, 12, bwd_p.at[partners])
    put(13, bwd_p, bwd_c, sibling)

    drain(rsem, 14, wrecv.at[pl.ds(0, width - 1)])
    wrecv[x_me] = jnp.zeros(wrecv.shape[1:], BF)
    total = wfull[x_me]
    for column in range(width):
        total = total + wrecv[column].astype(F32)
    wtot[x_me] = total.astype(BF)
    for k in x_order[:-1]:
        put(15, wtot.at[x_me], wtot.at[x_me], on_column(k))

    drain(rsem, 13, bwd_c)
    half_pipes = pipes // 2
    junc_grad = COUPLING * (
        dot(sel_b[:, 0:half_pipes], bwd_p[...].reshape(half_pipes, chans))
        + dot(sel_b[:, half_pipes:pipes], bwd_c[...].reshape(half_pipes, chans))
    )
    junc_act = jactv[...]
    gate = jax.nn.sigmoid(junc_act)
    act_grad = (junc_grad * (gate * (1.0 + junc_act * (1.0 - gate)))).astype(BF)
    jactv[...] = dot_nt(act_grad, jw_ref[...]).astype(BF).astype(F32)

    drain(rsem, 7, inbox.at[3, others])
    modes[...] = inbox[3].reshape(rows, chans)

    drain(rsem, 15, wtot.at[pl.ds(0, width - 1)])
    for column in range(width):
        cut = slice(column * share, (column + 1) * share)
        grv[cut, :] = wtot[column, 0].astype(F32)
        gmv[cut, :] = wtot[column, 1].astype(F32)
    for slot in range(4):
        drain(ssem, 2 * slot, duo.at[slot, :, 0])
        drain(ssem, 2 * slot + 1, inbox.at[slot, others])
    for phase, part in (
        (8, ag_z.at[0, pl.ds(0, line - 1)]),
        (9, fwd_p.at[partners]), (10, fwd_c),
        (11, ag_z.at[1, pl.ds(0, line - 1)]),
        (12, bwd_p.at[partners]), (13, bwd_c),
        (14, wrecv.at[pl.ds(0, width - 1)]), (15, wtot.at[pl.ds(0, width - 1)]),
    ):
        drain(ssem, phase, part)


def deliver(
    y_ref, local_ref, tab_ref, modes_ref, ends_ref, gr_ref, gm_ref,
    y_out, gi_out, gr_out, gm_out, giv, sems,
):
    copies = [
        pltpu.make_async_copy(source, target, sems.at[i])
        for i, (source, target) in enumerate(
            ((y_ref, y_out), (gr_ref, gr_out), (gm_ref, gm_out))
        )
    ]
    for copy in copies:
        copy.start()
    chunks = tab_ref.shape[0]
    tile_row = lax.broadcasted_iota(jnp.int32, (TILE, giv.shape[1]), 0)
    for k in range(chunks):
        part_rows = pl.ds(k * TILE, TILE)
        spread = dot(tab_ref[k], modes_ref[...])
        if k == 0:
            spread = spread + jnp.where(tile_row == 0, ends_ref[0:1, :], 0.0)
        if k == chunks - 1:
            spread = spread + jnp.where(tile_row == TILE - 1, ends_ref[1:2, :], 0.0)
        giv[part_rows, :] = (local_ref[part_rows, :] + spread.astype(BF).astype(F32)).astype(BF)
        copy = pltpu.make_async_copy(giv.at[part_rows], gi_out.at[part_rows], sems.at[3 + k])
        copy.start()
        copies.append(copy)
    for copy in copies:
        copy.wait()


def body(
    inputs, cotangent, point_weight, point_bias, spec_real, spec_imag,
    junc_weight, junc_bias, inlet_ids, outlet_ids,
):
    per_dev, cells, chans = inputs.shape
    len_count, width = lax.axis_size("len"), lax.axis_size("pipe")
    line, chips = LINE, len_count // CORES
    ys = chips // line
    rows, pipes = 2 * len_count, inlet_ids.shape[0]
    dims = dict(
        line=line, ys=ys, width=width, pipes=pipes, cells=cells, chans=chans, rows=rows
    )
    share = chans // width
    vm = pltpu.VMEM
    far = pl.BlockSpec(memory_space=pltpu.HBM)
    near = pl.BlockSpec(memory_space=pltpu.VMEM)
    results = (
        jax.ShapeDtypeStruct((cells, chans), BF),
        jax.ShapeDtypeStruct((cells, chans), BF),
        jax.ShapeDtypeStruct((chans, chans), F32),
        jax.ShapeDtypeStruct((chans, chans), F32),
    )
    chunks = cells // TILE
    made = pl.pallas_call(
        functools.partial(kernel_body, dims),
        out_shape=(
            results[0], jax.ShapeDtypeStruct((cells, chans), F32),
            jax.ShapeDtypeStruct((chunks, TILE, rows), BF),
            jax.ShapeDtypeStruct((rows, chans), BF), jax.ShapeDtypeStruct((8, chans), F32),
            results[2], results[3],
        ),
        in_specs=[far] * 10,
        out_specs=(near,) * 7,
        scratch_shapes=[
            vm((cells, chans), BF), vm((cells, chans), BF),
            vm((chans, chans), BF), vm((1, chans), F32), vm((chans, chans), BF),
            vm((chans, chans), BF), vm((chans, chans), BF), vm((1, chans), F32),
            vm((1, pipes), jnp.int32), vm((1, pipes), jnp.int32),
            vm((chunks, rows, TILE), BF), vm((cells, chans), F32), vm((cells, chans), BF),
            vm((rows, chans), F32),
            vm((4, chips, CORES, 2, chans), BF), vm((4, chips, CORES, 2, chans), BF),
            vm((4, chips, CORES, 2, chans), BF),
            vm((2, 2, chans), BF), vm((2, line, 2, chans), BF),
            vm((width * ys, 2 * line, chans), BF), vm((width * ys, 2 * line, chans), BF),
            vm((width * ys, line, chans), BF), vm((width * ys, line, chans), BF),
            vm((width, 2, share, chans), F32), vm((width, 2, share, chans), BF),
            vm((width, 2, share, chans), BF), vm((width, 2, share, chans), BF),
            vm((rows, rows), BF), vm((8, 2 * pipes), BF), vm((8, pipes), BF),
            vm((rows, chans), BF), vm((1, chans), F32),
            vm((2 * line, chans), F32),
            pltpu.SemaphoreType.DMA((10,)),
            pltpu.SemaphoreType.DMA((16,)), pltpu.SemaphoreType.DMA((16,)),
        ],
        compiler_params=pltpu.CompilerParams(
            collective_id=0, has_side_effects=True, vmem_limit_bytes=48 << 20
        ),
        name="operator_step",
    )(*(
        pltpu.with_memory_space_constraint(value, pltpu.HBM)
        for value in (
            inputs[0], cotangent[0], point_weight, point_bias[None, :], spec_real[0],
            spec_imag[0], junc_weight, junc_bias[None, :], inlet_ids[None, :],
            outlet_ids[None, :],
        )
    ))
    y, gi, gr, gm = pl.pallas_call(
        deliver,
        out_shape=results,
        in_specs=[near] * 7,
        out_specs=(far,) * 4,
        scratch_shapes=[vm((cells, chans), BF), pltpu.SemaphoreType.DMA((3 + chunks,))],
        compiler_params=pltpu.CompilerParams(vmem_limit_bytes=16 << 20),
        name="deliver",
    )(*(pltpu.with_memory_space_constraint(value, pltpu.VMEM) for value in made))
    return y[None], gi[None], gr[None], gm[None]


def solution(mesh):
    split = P(("len", "pipe"), None, None)
    modes = P("len", None, None)
    return jax.shard_map(
        body,
        mesh=mesh,
        in_specs=(split, split, P(), P(), modes, modes, P(), P(), P(), P()),
        out_specs=(split, split, modes, modes),
        check_vma=False,
    )
```

```python
import functools
import math

import jax
import jax.numpy as jnp
from jax import lax
from jax.experimental import pallas as pl
from jax.experimental.pallas import tpu as pltpu
from jax.sharding import PartitionSpec as P

COUPLING = 0.125
LINE = 16
CORES = 2
FAR = 5
TILE = 256
MESH = pl.DeviceIdType.MESH
BF = jnp.bfloat16
F32 = jnp.float32
GELU_A = math.sqrt(2.0 / math.pi)
GELU_B = GELU_A * 0.044715


def dot(left, right):
    return jnp.dot(left, right, preferred_element_type=F32)


def dot_nt(left, right):
    return lax.dot_general(left, right, (((1,), (1,)), ((), ())), preferred_element_type=F32)


def dot_tn(left, right):
    return lax.dot_general(left, right, (((0,), (0,)), ((), ())), preferred_element_type=F32)


def turn_cos(index, cell_count):
    half, quarter = cell_count // 2, cell_count // 4
    away = jnp.abs(index - half)
    folded = jnp.minimum(away, half - away)
    x = folded.astype(F32) * (2.0 * math.pi / cell_count)
    y = x * x
    value = jnp.full_like(y, 1.0 / math.factorial(12))
    for power in (10, 8, 6, 4, 2, 0):
        sign = 1.0 if power % 4 == 0 else -1.0
        value = value * y + sign / math.factorial(power)
    return jnp.where(away > quarter, value, -value)


def base_tables(row, col, cell_count):
    index = row // 2 * col + (cell_count // 4) * (row % 2)
    scale = 1.0 / math.sqrt(cell_count)
    cosine = turn_cos(index % cell_count, cell_count) * scale
    sine = turn_cos((index + 3 * (cell_count // 4)) % cell_count, cell_count) * scale
    return cosine, sine


def shift_factors(row, step, steps):
    index = (row // 2 * step) % steps
    return turn_cos(index, steps), turn_cos((index + 3 * (steps // 4)) % steps, steps)


def kernel_body(
    dims,
    x_hbm, cot_hbm, pw_hbm, pb_hbm, sr_hbm, si_hbm, jw_hbm, jb_hbm, in_hbm, out_hbm,
    yv, localv, ttab, modes, jactv, grv, gmv,
    xv, cotv, pw_ref, pb_ref, sr_ref, si_ref, jw_ref, jb_ref, in_ref, out_ref,
    ftab, pointv, gtv, acc,
    outbox, duo, inbox,
    own_z, ag_z, fwd_p, fwd_c, bwd_p, bwd_c,
    wfull, wsend, wrecv, wtot,
    perm_q, sel_f, sel_b, scaledv, condv, rowv,
    load_sem, ssem, rsem,
):
    line, ys, width, pipes = dims["line"], dims["ys"], dims["width"], dims["pipes"]
    cells, chans, rows = dims["cells"], dims["chans"], dims["rows"]
    chips = line * ys
    chunks = cells // TILE
    len_me, x_me = lax.axis_index("len"), lax.axis_index("pipe")
    c_me = len_me % CORES
    chip_me = len_me // CORES
    z_me = chip_me % line
    y_me = chip_me // line
    c_other = 1 - c_me

    def chip_at(dy, dz):
        return (y_me + dy) % ys * line + (z_me + dz) % line

    def on_chip(chip, core=None):
        return {"len": chip * CORES + (c_me if core is None else core), "pipe": x_me}

    def on_column(k):
        return {"len": len_me, "pipe": (x_me + k) % width}

    def on_plane(dy, k):
        return {"len": chip_at(dy, 0) * CORES + c_me, "pipe": (x_me + k) % width}

    sibling = {"len": chip_me * CORES + c_other, "pipe": x_me}
    y_order = sorted(range(ys), key=lambda k: -min(k, ys - k))
    x_order = sorted(range(width), key=lambda k: -min(k, width - k))
    plane = [(dy, k) for dy in y_order for k in x_order][:-1]

    def z_step(j):
        return line // 2 + ((j + 1) // 2) * (1 - 2 * (j % 2))

    def put(phase, source, target, device):
        pltpu.make_async_remote_copy(
            src_ref=source, dst_ref=target, send_sem=ssem.at[phase], recv_sem=rsem.at[phase],
            device_id=device, device_id_type=MESH,
        ).start()

    def drain(sem, phase, part):
        pltpu.make_async_copy(part, part, sem.at[phase]).wait()

    def each_chip(action, low, high):
        def step(j, carry):
            for dy in y_order:
                action(chip_at(dy, z_step(j)))
            return carry

        lax.fori_loop(low, min(high, line - 1), step, 0)
        if high == line:
            for dy in y_order[:-1]:
                action(chip_at(dy, 0))

    barrier = pltpu.get_barrier_semaphore()

    def greet(device):
        pl.semaphore_signal(barrier, inc=1, device_id=device, device_id_type=MESH)

    def greet_both(chip):
        greet(on_chip(chip))
        greet(on_chip(chip, c_other))

    each_chip(greet_both, 0, FAR)
    each_chip(lambda chip: greet(on_chip(chip)), FAR, line)
    for dy, k in plane:
        if k:
            greet(on_plane(dy, k))
    greet(sibling)

    loads = [
        pltpu.make_async_copy(source, target, load_sem.at[i])
        for i, (source, target) in enumerate((
            (x_hbm, xv), (sr_hbm, sr_ref), (si_hbm, si_ref), (in_hbm, in_ref), (out_hbm, out_ref),
            (pw_hbm, pw_ref), (pb_hbm, pb_ref), (jw_hbm, jw_ref), (jb_hbm, jb_ref), (cot_hbm, cotv),
        ))
    ]
    for load in loads:
        load.start()

    row_id = lax.broadcasted_iota(jnp.int32, (rows, TILE), 0)
    col_id = lax.broadcasted_iota(jnp.int32, (rows, TILE), 1)
    base_cos, base_sin = base_tables(row_id, col_id, cells)
    localv[0:rows, :] = base_cos
    localv[rows : 2 * rows, :] = base_sin
    row_one = lax.broadcasted_iota(jnp.int32, (rows, 1), 0)
    doubled = jnp.where(row_one < 2, 1.0, 2.0)
    acc[...] = jnp.zeros_like(acc)
    loads[0].wait()

    def spectra_step(k, carry):
        turn_c, turn_s = shift_factors(row_one, k, chunks)
        table = (localv[0:rows, :] * turn_c - localv[rows : 2 * rows, :] * turn_s).astype(BF)
        ftab[k] = table
        acc[...] += dot(table, xv[pl.ds(k * TILE, TILE), :])
        return carry

    lax.fori_loop(0, chunks, spectra_step, 0)
    outbox[0] = acc[...].astype(BF).reshape(chips, CORES, 2, chans)
    cell_id = lax.broadcasted_iota(jnp.int32, (TILE, rows), 0)
    mode_id = lax.broadcasted_iota(jnp.int32, (TILE, rows), 1)
    side_cos, side_sin = base_tables(mode_id, cell_id, cells)
    localv[0:TILE, :] = side_cos
    localv[TILE : 2 * TILE, :] = side_sin
    col_one = lax.broadcasted_iota(jnp.int32, (1, rows), 1)

    def side_step(k, carry):
        turn_c, turn_s = shift_factors(col_one, k, chunks)
        ttab[k] = (localv[0:TILE, :] * turn_c - localv[TILE : 2 * TILE, :] * turn_s).astype(BF)
        return carry

    lax.fori_loop(0, chunks, side_step, 0)

    to_row = lax.broadcasted_iota(jnp.int32, (rows, rows), 0)
    from_row = lax.broadcasted_iota(jnp.int32, (rows, rows), 1)
    swapped = jnp.where(to_row % 2 == 0, to_row + 1, to_row - 1)
    sign = jnp.where(to_row % 2 == 0, -1.0, 1.0)
    perm_q[...] = jnp.where(from_row == swapped, sign, 0.0).astype(BF)
    pl.semaphore_wait(barrier, chips - 1 + FAR * ys + ys * (width - 1) + 1)

    def exchange(slot, between=None):
        phase = 2 * slot
        put(phase, outbox.at[slot, :, c_other], duo.at[slot, :, c_me], sibling)

        def direct(chip):
            for core in (c_me, c_other):
                put(
                    phase + 1, outbox.at[slot, chip, core], inbox.at[slot, chip_me, c_me],
                    on_chip(chip, core),
                )

        def paired(chip):
            put(phase + 1, duo.at[slot, chip], inbox.at[slot, chip_me], on_chip(chip))

        each_chip(direct, 0, FAR)
        duo[slot, :, c_me] = outbox[slot, :, c_me]
        if between is not None:
            between()
        drain(rsem, phase, duo.at[slot, :, 0])
        each_chip(paired, FAR, line)
        inbox[slot, chip_me] = duo[slot, chip_me]

    others = pl.ds(0, chips - 1)

    def gather_z(slot, phase, first, second):
        part = lax.broadcasted_iota(jnp.int32, (2, chans), 0)
        own_z[slot] = jnp.where(part == 0, first, second).astype(BF)
        ag_z[slot, z_me] = own_z[slot]

        def step(j, carry):
            put(phase, own_z.at[slot], ag_z.at[slot, z_me], on_chip(chip_at(0, z_step(j))))
            return carry

        lax.fori_loop(0, line - 1, step, 0)

    def gather_plane(ref, phase, block):
        here = x_me * ys + y_me
        ref[here] = block
        for dy, k in plane:
            put(phase, ref.at[here], ref.at[here], on_plane(dy, k))

    partners = pl.ds(0, len(plane))

    first_row = xv[0:16, :].astype(F32)[0:1, :]
    last_row = xv[cells - 16 : cells, :].astype(F32)[15:16, :]
    exchange(0, lambda: gather_z(0, 8, first_row, last_row))

    for load in loads[1:9]:
        load.wait()

    ids_in, ids_out = in_ref[...].astype(F32), out_ref[...].astype(F32)
    place = lax.broadcasted_iota(jnp.int32, (1, pipes), 1)
    here = place == len_me * width + x_me
    mine_in = jnp.sum(jnp.where(here, ids_in, 0.0), axis=1, keepdims=True)
    mine_out = jnp.sum(jnp.where(here, ids_out, 0.0), axis=1, keepdims=True)
    which = lax.broadcasted_iota(jnp.int32, (8, pipes), 0)

    def matches(ids):
        pair = jnp.where(which == 0, (ids == mine_in).astype(F32), (ids == mine_out).astype(F32))
        return jnp.where(which < 2, pair, 0.0).astype(BF)

    def pipe_of(index):
        chip = index % chips
        column = (index // chips) % width
        core = jnp.where(index // (chips * width) == 0, c_me, c_other)
        return (chip * CORES + core) * width + column

    match_in, match_out = matches(ids_in), matches(ids_out)
    entry = lax.broadcasted_iota(jnp.int32, (1, 2 * pipes), 1)
    pipe_e = pipe_of(entry // 2)
    pipe_row = lax.broadcasted_iota(jnp.int32, (pipes, 2 * pipes), 0)
    hot_first = jnp.where(pipe_row == jnp.where(entry % 2 == 0, pipe_e, -1), 1.0, 0.0).astype(BF)
    hot_last = jnp.where(pipe_row == jnp.where(entry % 2 == 1, pipe_e, -1), 1.0, 0.0).astype(BF)
    sel_f[...] = (dot(match_in, hot_first) + dot(match_out, hot_last)).astype(BF)
    entry = lax.broadcasted_iota(jnp.int32, (1, pipes), 1)
    pipe_row = lax.broadcasted_iota(jnp.int32, (pipes, pipes), 0)
    hot = jnp.where(pipe_row == pipe_of(entry), 1.0, 0.0).astype(BF)
    sel_b[...] = (dot(match_in, hot) + dot(match_out, hot)).astype(BF)

    drain(rsem, 8, ag_z.at[0, pl.ds(0, line - 1)])
    for spot in range(line):
        rowv[2 * spot : 2 * spot + 2, :] = ag_z[0, spot].astype(F32)
    gather_plane(fwd_p, 9, rowv[...].astype(BF))

    drain(rsem, 1, inbox.at[0, others])
    seen = inbox[0].reshape(rows, chans)
    turned = dot(perm_q[...], seen).astype(BF)
    mixed = dot(seen, sr_ref[...]) + dot(turned, si_ref[...])
    outbox[1] = mixed.astype(BF).reshape(chips, CORES, 2, chans)
    exchange(1)
    drain(rsem, 9, fwd_p.at[partners])
    put(10, fwd_p, fwd_c, sibling)

    def point_step(k, carry):
        part_rows = pl.ds(k * TILE, TILE)
        pointv[part_rows, :] = dot(xv[part_rows, :], pw_ref[...]) + pb_ref[...]
        return carry

    lax.fori_loop(0, chunks, point_step, 0)

    drain(rsem, 10, fwd_c)
    sums = dot(sel_f[:, 0:pipes], fwd_p[...].reshape(pipes, chans)) + dot(
        sel_f[:, pipes : 2 * pipes], fwd_c[...].reshape(pipes, chans)
    )
    junc_act = dot(sums.astype(BF), jw_ref[...]) + jb_ref[...]
    jactv[...] = junc_act
    junc_rows = (junc_act * jax.nn.sigmoid(junc_act)).astype(BF).astype(F32)
    condv[...] = COUPLING * (junc_rows[0:1, :] + junc_rows[1:2, :])
    loads[9].wait()

    drain(rsem, 3, inbox.at[1, others])
    scaledv[...] = (inbox[1].reshape(rows, chans).astype(F32) * doubled).astype(BF)

    acc[...] = jnp.zeros_like(acc)

    def gelu_step(k, total):
        part_rows = pl.ds(k * TILE, TILE)
        spectral = dot(ttab[k], scaledv[...])
        pre = (spectral + condv[...]).astype(BF).astype(F32)
        s = pointv[part_rows, :] + pre
        square = s * s
        half = 0.5 + 0.5 * jnp.tanh(s * (GELU_A + GELU_B * square))
        value = s * half
        yv[part_rows, :] = value.astype(BF)
        slope = half + (value - value * half) * (2.0 * GELU_A + (6.0 * GELU_B) * square)
        grad = (cotv[part_rows, :].astype(F32) * slope).astype(BF)
        gtv[part_rows, :] = grad
        acc[...] += dot(ftab[k], grad)
        return total + jnp.sum(grad.astype(F32), axis=0, keepdims=True)

    grad_cond = lax.fori_loop(0, chunks, gelu_step, jnp.zeros((1, chans), F32), unroll=True)
    outbox[2] = (acc[...] * doubled).astype(BF).reshape(chips, CORES, 2, chans)
    high = grad_cond.astype(BF).astype(F32)
    gather_z(1, 11, high, grad_cond - high)
    exchange(2)
    def local_step(k, carry):
        part_rows = pl.ds(k * TILE, TILE)
        localv[part_rows, :] = dot_nt(gtv[part_rows, :], pw_ref[...])
        return carry

    lax.fori_loop(0, chunks, local_step, 0)

    drain(rsem, 11, ag_z.at[1, pl.ds(0, line - 1)])
    for spot in range(line):
        rowv[spot : spot + 1, :] = jnp.sum(ag_z[1, spot].astype(F32), axis=0, keepdims=True)
    gather_plane(bwd_p, 12, rowv[0:line, :].astype(BF))

    drain(rsem, 5, inbox.at[2, others])
    grads = inbox[2].reshape(rows, chans)
    flipped = dot_tn(perm_q[...], grads).astype(BF)
    returned = dot_nt(grads, sr_ref[...]) + dot_nt(flipped, si_ref[...])
    outbox[3] = returned.astype(BF).reshape(chips, CORES, 2, chans)
    share = chans // width

    def weight_terms():
        seen = inbox[0].reshape(rows, chans)
        real = dot_tn(seen, grads)
        imag = dot_tn(seen, flipped)
        for column in range(width):
            cut = slice(column * share, (column + 1) * share)
            wfull[column, 0] = real[cut, :]
            wfull[column, 1] = imag[cut, :]
        wsend[...] = wfull[...].astype(BF)
        for k in x_order[:-1]:
            put(14, wsend.at[(x_me + k) % width], wrecv.at[x_me], on_column(k))

    exchange(3, weight_terms)
    drain(rsem, 12, bwd_p.at[partners])
    put(13, bwd_p, bwd_c, sibling)

    drain(rsem, 14, wrecv.at[pl.ds(0, width - 1)])
    wrecv[x_me] = jnp.zeros(wrecv.shape[1:], BF)
    total = wfull[x_me]
    for column in range(width):
        total = total + wrecv[column].astype(F32)
    wtot[x_me] = total.astype(BF)
    for k in x_order[:-1]:
        put(15, wtot.at[x_me], wtot.at[x_me], on_column(k))

    drain(rsem, 13, bwd_c)
    half_pipes = pipes // 2
    junc_grad = COUPLING * (
        dot(sel_b[:, 0:half_pipes], bwd_p[...].reshape(half_pipes, chans))
        + dot(sel_b[:, half_pipes:pipes], bwd_c[...].reshape(half_pipes, chans))
    )
    junc_act = jactv[...]
    gate = jax.nn.sigmoid(junc_act)
    act_grad = (junc_grad * (gate * (1.0 + junc_act * (1.0 - gate)))).astype(BF)
    jactv[...] = dot_nt(act_grad, jw_ref[...]).astype(BF).astype(F32)

    drain(rsem, 7, inbox.at[3, others])
    modes[...] = inbox[3].reshape(rows, chans)

    drain(rsem, 15, wtot.at[pl.ds(0, width - 1)])
    for column in range(width):
        cut = slice(column * share, (column + 1) * share)
        grv[cut, :] = wtot[column, 0].astype(F32)
        gmv[cut, :] = wtot[column, 1].astype(F32)
    for slot in range(4):
        drain(ssem, 2 * slot, duo.at[slot, :, 0])
        drain(ssem, 2 * slot + 1, inbox.at[slot, others])
    for phase, part in (
        (8, ag_z.at[0, pl.ds(0, line - 1)]),
        (9, fwd_p.at[partners]), (10, fwd_c),
        (11, ag_z.at[1, pl.ds(0, line - 1)]),
        (12, bwd_p.at[partners]), (13, bwd_c),
        (14, wrecv.at[pl.ds(0, width - 1)]), (15, wtot.at[pl.ds(0, width - 1)]),
    ):
        drain(ssem, phase, part)


def deliver(
    y_ref, local_ref, tab_ref, modes_ref, ends_ref, gr_ref, gm_ref,
    y_out, gi_out, gr_out, gm_out, giv, sems,
):
    copies = [
        pltpu.make_async_copy(source, target, sems.at[i])
        for i, (source, target) in enumerate(
            ((y_ref, y_out), (gr_ref, gr_out), (gm_ref, gm_out))
        )
    ]
    for copy in copies:
        copy.start()
    chunks = tab_ref.shape[0]
    tile_row = lax.broadcasted_iota(jnp.int32, (TILE, giv.shape[1]), 0)
    for k in range(chunks):
        part_rows = pl.ds(k * TILE, TILE)
        spread = dot(tab_ref[k], modes_ref[...])
        if k == 0:
            spread = spread + jnp.where(tile_row == 0, ends_ref[0:1, :], 0.0)
        if k == chunks - 1:
            spread = spread + jnp.where(tile_row == TILE - 1, ends_ref[1:2, :], 0.0)
        giv[part_rows, :] = (local_ref[part_rows, :] + spread.astype(BF).astype(F32)).astype(BF)
        copy = pltpu.make_async_copy(giv.at[part_rows], gi_out.at[part_rows], sems.at[3 + k])
        copy.start()
        copies.append(copy)
    for copy in copies:
        copy.wait()


def body(
    inputs, cotangent, point_weight, point_bias, spec_real, spec_imag,
    junc_weight, junc_bias, inlet_ids, outlet_ids,
):
    per_dev, cells, chans = inputs.shape
    len_count, width = lax.axis_size("len"), lax.axis_size("pipe")
    line, chips = LINE, len_count // CORES
    ys = chips // line
    rows, pipes = 2 * len_count, inlet_ids.shape[0]
    dims = dict(
        line=line, ys=ys, width=width, pipes=pipes, cells=cells, chans=chans, rows=rows
    )
    share = chans // width
    vm = pltpu.VMEM
    far = pl.BlockSpec(memory_space=pltpu.HBM)
    near = pl.BlockSpec(memory_space=pltpu.VMEM)
    results = (
        jax.ShapeDtypeStruct((cells, chans), BF),
        jax.ShapeDtypeStruct((cells, chans), BF),
        jax.ShapeDtypeStruct((chans, chans), F32),
        jax.ShapeDtypeStruct((chans, chans), F32),
    )
    chunks = cells // TILE
    made = pl.pallas_call(
        functools.partial(kernel_body, dims),
        out_shape=(
            results[0], jax.ShapeDtypeStruct((cells, chans), F32),
            jax.ShapeDtypeStruct((chunks, TILE, rows), BF),
            jax.ShapeDtypeStruct((rows, chans), BF), jax.ShapeDtypeStruct((8, chans), F32),
            results[2], results[3],
        ),
        in_specs=[far] * 10,
        out_specs=(near,) * 7,
        scratch_shapes=[
            vm((cells, chans), BF), vm((cells, chans), BF),
            vm((chans, chans), BF), vm((1, chans), F32), vm((chans, chans), BF),
            vm((chans, chans), BF), vm((chans, chans), BF), vm((1, chans), F32),
            vm((1, pipes), jnp.int32), vm((1, pipes), jnp.int32),
            vm((chunks, rows, TILE), BF), vm((cells, chans), F32), vm((cells, chans), BF),
            vm((rows, chans), F32),
            vm((4, chips, CORES, 2, chans), BF), vm((4, chips, CORES, 2, chans), BF),
            vm((4, chips, CORES, 2, chans), BF),
            vm((2, 2, chans), BF), vm((2, line, 2, chans), BF),
            vm((width * ys, 2 * line, chans), BF), vm((width * ys, 2 * line, chans), BF),
            vm((width * ys, line, chans), BF), vm((width * ys, line, chans), BF),
            vm((width, 2, share, chans), F32), vm((width, 2, share, chans), BF),
            vm((width, 2, share, chans), BF), vm((width, 2, share, chans), BF),
            vm((rows, rows), BF), vm((8, 2 * pipes), BF), vm((8, pipes), BF),
            vm((rows, chans), BF), vm((1, chans), F32),
            vm((2 * line, chans), F32),
            pltpu.SemaphoreType.DMA((10,)),
            pltpu.SemaphoreType.DMA((16,)), pltpu.SemaphoreType.DMA((16,)),
        ],
        compiler_params=pltpu.CompilerParams(
            collective_id=0, has_side_effects=True, vmem_limit_bytes=48 << 20
        ),
        name="operator_step",
    )(*(
        pltpu.with_memory_space_constraint(value, pltpu.HBM)
        for value in (
            inputs[0], cotangent[0], point_weight, point_bias[None, :], spec_real[0],
            spec_imag[0], junc_weight, junc_bias[None, :], inlet_ids[None, :],
            outlet_ids[None, :],
        )
    ))
    y, gi, gr, gm = pl.pallas_call(
        deliver,
        out_shape=results,
        in_specs=[near] * 7,
        out_specs=(far,) * 4,
        scratch_shapes=[vm((cells, chans), BF), pltpu.SemaphoreType.DMA((3 + chunks,))],
        compiler_params=pltpu.CompilerParams(vmem_limit_bytes=16 << 20),
        name="deliver",
    )(*(pltpu.with_memory_space_constraint(value, pltpu.VMEM) for value in made))
    return y[None], gi[None], gr[None], gm[None]


def solution(mesh):
    split = P(("len", "pipe"), None, None)
    modes = P("len", None, None)
    return jax.shard_map(
        body,
        mesh=mesh,
        in_specs=(split, split, P(), P(), modes, modes, P(), P(), P(), P()),
        out_specs=(split, split, modes, modes),
        check_vma=False,
    )
```
